32 devices in a mesh: mem: 2 (over x), gy: 4 (over z), gx: 4 (over y, core).
Axes of the slice: x: 2, y: 2, z: 4, core: 2. Of those that a mesh axis runs over, the one named last changes fastest.
Arguments:
- alpha: float32 [16, 32, 64, 512], P('mem', None, 'gy', 'gx'), may hold values from -4 to 4
- perturb: bfloat16 [16, 4, 32, 64, 512], P('mem', None, None, 'gy', 'gx'), may hold values from -6 to 6
- chi: float32 [4, 32, 64, 512], P(None, None, 'gy', 'gx'), may hold values from -4 to 4
- kappa: float32 [64, 512], P('gy', 'gx'), may hold values from 0.05 to 0.24
- vert_bounds: int32 [2, 32], replicated, may hold values from 0 to 31, as said below
- static_vert: float32 [4, 32, 32], replicated, may hold values from -1 to 1
- fine_owner: int32 [16, 2], P(('gy', 'gx')), may hold values from 0 to 1, each once within a row
- obs_stencil: int32 [32768], P(('mem', 'gy', 'gx')), may hold values from 0 to 959
- obs_weight: float32 [4, 32768], P(None, ('mem', 'gy', 'gx')), may hold values from 0.05 to 0.5
- background: bfloat16 [32768, 128], P(('mem', 'gy', 'gx')), may hold values from -6 to 6
- observed: float32 [8, 32768], P(None, ('mem', 'gy', 'gx')), may hold values from -6 to 6
- inv_var: float32 [8, 32768], P(None, ('mem', 'gy', 'gx')), may hold values from 2 to 32
- jacobian: float32 [8, 128], replicated, may hold values from -0.5 to 0.5
- obs_count: int32 [32], P(('mem', 'gy', 'gx')), may hold values from 256 to 1024, as said below
Outputs:
- grad_alpha: float32 [16, 32, 64, 512], P('mem', None, 'gy', 'gx')
- grad_chi: float32 [4, 32, 64, 512], P(None, None, 'gy', 'gx')
The draws below stay inside these ranges and needn't reach their ends.
Inputs may be any that keep to these rules, and one draw needn't show every extreme that they name: `vert_bounds`: row 0 holds each level's lowest and row 1 its highest coupled level; level l lies between both inclusive, and each lies 1 to 4 levels from l unless cut at the ends of the column. `obs_count`: observations below this count in a device's block are live; some device has exactly 1024 and some exactly 256.
All inputs are finite; a program needn't handle non-finite values.
Results may differ from the reference program's by a relative error of at most 0.00099.
Values may be sent and summed in bfloat16 or wider, within the bound.
A program may use at most 128 MiB of HBM per device.

```python
import math
import jax
import jax.numpy as jnp
from jax import lax

MEMBERS = 16
L = 32
V = 4
VL = 128
TY = 16
TX = 128
NY = 64
NX = 512
TILES = 16
FB = 64
SHIFT = 32
NDIFF = 4
VREACH = 4
OBS_DEV = 1024
OBS_TOTAL = 32768
NCHAN = 8
N_MEM = 2
N_GX = 4
DEVICES = 32


def draw_vert_bounds(key, part):
    key_low, key_high = jax.random.split(jax.random.fold_in(key, 11))
    level = jnp.arange(L, dtype=jnp.int32)
    lower = jnp.maximum(level - jax.random.randint(key_low, (L,), 1, VREACH + 1), 0)
    upper = jnp.minimum(level + jax.random.randint(key_high, (L,), 1, VREACH + 1), L - 1)
    return jnp.stack([lower, upper]).astype(jnp.int32)


def draw_obs_count(key, part):
    key_count, key_pick = jax.random.split(jax.random.fold_in(key, 23))
    counts = jax.random.randint(key_count, (DEVICES,), OBS_DEV // 4, OBS_DEV + 1)
    order = jax.random.permutation(key_pick, DEVICES)
    counts = counts.at[order[0]].set(OBS_DEV).at[order[1]].set(OBS_DEV // 4)
    return counts.astype(jnp.int32)


def plant(result, stream_key, least, largest):
    longest = result.shape.index(max(result.shape))
    spots = []
    for shift in (0, 1):
        where = [jax.random.randint(jax.random.fold_in(stream_key, axis), (), 0, length) for axis, length in enumerate(result.shape)]
        where[longest] = (where[longest] + shift) % result.shape[longest]
        spots.append(tuple(where))
    return result.at[spots[0]].set(least).at[spots[1]].set(largest)


def level_of(own_key, extent, pieces, low, top_value):
    def one(dim, parts):
        draws = jax.random.uniform(jax.random.fold_in(jax.random.fold_in(own_key, 6), dim), (parts,), jnp.float32, low / len(pieces), top_value / len(pieces))
        return jnp.repeat(jnp.exp(draws), extent[dim] // parts).reshape((-1,) + (1,) * (len(extent) - dim - 1))

    gain = one(*pieces[0])
    for cut in pieces[1:]:
        gain = gain * one(*cut)
    return gain


def normal_values(rng, extent, width, limit, cuts=(), kind=jnp.bfloat16):
    result = width * jax.random.normal(rng, extent, jnp.float32)
    if cuts:
        result = result * level_of(rng, extent, cuts, -0.22, 0.18)
    return jnp.clip(result, -limit, limit).astype(kind)


def setup_inputs(seed: int = 0) -> dict:
    key_of = jax.random.split(jax.random.key(seed), 15)
    return {
        "alpha": normal_values(key_of[0], (MEMBERS, L, NY, NX), 0.5, 4.0, ((0, 2), (2, 4), (3, 4)), jnp.float32),
        "perturb": normal_values(key_of[1], (MEMBERS, V, L, NY, NX), 1.0, 6.0, ((0, 2), (3, 4), (4, 4))),
        "chi": normal_values(key_of[2], (V, L, NY, NX), 0.5, 4.0, ((2, 4), (3, 4)), jnp.float32),
        "kappa": jnp.clip(jnp.exp(math.log(0.24) - 1.5686159 * jax.random.uniform(key_of[3], (NY, NX), jnp.float32) ** level_of(key_of[3], (NY, NX), ((0, 4), (1, 4)), -0.2, 0.2)), 0.05, 0.24),
        "vert_bounds": draw_vert_bounds(jax.random.fold_in(key_of[14], 71), 0),
        "static_vert": normal_values(key_of[5], (V, L, L), L ** -0.5, 1.0, (), jnp.float32),
        "fine_owner": jax.vmap(lambda own: jax.random.permutation(own, N_MEM))(jax.random.split(key_of[6], TILES)).reshape((TILES, N_MEM)).astype(jnp.int32),
        "obs_stencil": plant(jax.random.randint(key_of[7], (OBS_TOTAL,), 0, (TY - 1) * FB), jax.random.fold_in(key_of[7], 1), 0, ((TY - 1) * FB) - 1).astype(jnp.int32),
        "obs_weight": jnp.clip(0.05 + 0.45 * jax.random.uniform(key_of[8], (4, OBS_TOTAL), jnp.float32) ** level_of(key_of[8], (4, OBS_TOTAL), ((1, 32),), -0.2, 0.2), 0.05, 0.5),
        "background": normal_values(key_of[9], (OBS_TOTAL, VL), 1.0, 6.0, ((0, 32),)),
        "observed": normal_values(key_of[10], (NCHAN, OBS_TOTAL), 1.0, 6.0, ((1, 32),), jnp.float32),
        "inv_var": jnp.clip(jnp.exp(math.log(32.0) - 2.7725887 * jax.random.uniform(key_of[11], (NCHAN, OBS_TOTAL), jnp.float32) ** level_of(key_of[11], (NCHAN, OBS_TOTAL), ((1, 32),), -0.2, 0.2)), 2.0, 32.0),
        "jacobian": normal_values(key_of[12], (NCHAN, VL), VL ** -0.5, 0.5, (), jnp.float32),
        "obs_count": draw_obs_count(jax.random.fold_in(key_of[14], 71), 0),
    }


ensemble_weight = 0.8
static_weight = 0.6
vertical_scale = 2.0
highest = lax.Precision.HIGHEST

def vertical_matrix(vert_bounds, levels):
    row_level = lax.broadcasted_iota(jnp.int32, (levels, levels), 0)
    col_level = lax.broadcasted_iota(jnp.int32, (levels, levels), 1)
    inside = (col_level >= vert_bounds[0][:, None]) & (col_level <= vert_bounds[1][:, None])
    distance = jnp.abs(row_level - col_level).astype(jnp.float32)
    return jnp.where(inside, jnp.exp(-distance / vertical_scale), jnp.zeros_like(distance))

def laplace(values):
    from_north = jnp.concatenate([values[:, :, :1], values[:, :, :-1]], axis=2)
    from_south = jnp.concatenate([values[:, :, 1:], values[:, :, -1:]], axis=2)
    return from_north + from_south + jnp.roll(values, 1, axis=3) + jnp.roll(values, -1, axis=3) - 4.0 * values

def reference(alpha, perturb, chi, kappa, vert_bounds, static_vert, fine_owner, obs_stencil, obs_weight, background, observed, inv_var, jacobian, obs_count):
    column_width = V * L
    ens_scale = ensemble_weight / math.sqrt(MEMBERS - 1)
    vertical = vertical_matrix(vert_bounds, L)
    spread = jnp.einsum('lm,kmyx->klyx', vertical, alpha, precision=highest)
    for repeat in range(NDIFF):
        spread = spread + kappa * laplace(spread)

    def add_member(carry, paired):
        member_pert, member_spread = paired
        return (carry + member_pert.astype(jnp.float32) * member_spread[None], 0)
    member_total, unused = lax.scan(add_member, jnp.zeros((V, L, NY, NX), jnp.float32), (perturb, spread))
    static = jnp.einsum('vlm,vmyx->vlyx', static_vert, chi, precision=highest)
    increment = (ens_scale * member_total + static_weight * static).astype(jnp.bfloat16)
    flat_increment = increment.reshape(column_width, NY * NX)
    obs_index = jnp.arange(OBS_TOTAL, dtype=jnp.int32)
    obs_device = (obs_index // OBS_DEV).astype(jnp.int32)
    member_group = (obs_device // TILES).astype(jnp.int32)
    tile_index = (obs_device % TILES).astype(jnp.int32)
    owners = fine_owner[tile_index]
    band_ids = lax.broadcasted_iota(jnp.int32, owners.shape, 1)
    band_index = lax.optimization_barrier(jnp.sum(jnp.where(owners == member_group[:, None], band_ids, jnp.zeros_like(band_ids)), axis=1)).astype(jnp.int32)
    anchor_row = (obs_stencil // FB).astype(jnp.int32)
    anchor_col = (obs_stencil % FB).astype(jnp.int32)
    base_row = tile_index // N_GX * TY + anchor_row
    base_col = tile_index % N_GX * TX + band_index * FB + SHIFT + anchor_col
    cells_of = jnp.stack([((base_row + corner // 2) * NX + (base_col + corner % 2) % NX).astype(jnp.int32) for corner in range(4)])
    increment_obs = jnp.zeros((OBS_TOTAL, column_width), jnp.float32)
    for corner in range(4):
        picked = jnp.take(flat_increment, cells_of[corner], axis=1).T.astype(jnp.float32)
        increment_obs = increment_obs + obs_weight[corner][:, None] * picked
    bent = jnp.tanh(background.astype(jnp.float32) + increment_obs)
    modeled = jnp.einsum('cv,ov->co', jacobian, bent, precision=highest)
    live = obs_index % OBS_DEV < obs_count[obs_device]
    misfit = jnp.where(live[None, :], (modeled - observed) * inv_var, jnp.zeros_like(modeled))
    state_grad = (1.0 - bent * bent) * jnp.einsum('co,cv->ov', misfit, jacobian, precision=highest)
    global_grad = jnp.zeros((column_width, NY * NX), jnp.float32)
    for corner in range(4):
        global_grad = global_grad.at[:, cells_of[corner]].add((obs_weight[corner][:, None] * state_grad).T)
    gradient = global_grad.reshape(V, L, NY, NX)
    grad_chi = chi + static_weight * jnp.einsum('vlm,vlyx->vmyx', static_vert, gradient, precision=highest)

    def member_back(member_pert):
        return ens_scale * lax.optimization_barrier(jnp.sum(member_pert.astype(jnp.float32) * gradient, axis=0))
    back_spread = lax.map(member_back, perturb)
    for repeat in range(NDIFF):
        back_spread = back_spread + laplace(kappa * back_spread)
    grad_alpha = alpha + jnp.einsum('lm,klyx->kmyx', vertical, back_spread, precision=highest)
    return (grad_alpha, grad_chi)
```

```python
import math

import jax
import jax.numpy as jnp
from jax import lax
from jax.experimental import pallas as pl
from jax.experimental.pallas import tpu as pltpu
from jax.sharding import PartitionSpec as P

NDIFF = 4

ensemble_weight = 0.8
static_weight = 0.6
vertical_scale = 2.0
highest = lax.Precision.HIGHEST
f32 = jnp.float32
bf16 = jnp.bfloat16
NT = (((1,), (1,)), ((), ()))
TN = (((0,), (0,)), ((), ()))


def shifted(value, axis, steps):
    count = lax.axis_size(axis)
    pairs = [(source, (source + steps) % count) for source in range(count)]
    return lax.ppermute(value, axis, pairs)


def params(grid_dims=0):
    if grid_dims:
        return pltpu.CompilerParams(
            dimension_semantics=("arbitrary",) * grid_dims, vmem_limit_bytes=56 << 20
        )
    return pltpu.CompilerParams(vmem_limit_bytes=56 << 20)


SIDE = 8
NN = (((1,), (0,)), ((), ()))


def compass():
    gx, gy = lax.axis_index("gx"), lax.axis_index("gy")
    gx_count, gy_count = lax.axis_size("gx"), lax.axis_size("gy")
    east, west = lax.rem(gx + 1, gx_count), lax.rem(gx + gx_count - 1, gx_count)
    return east, west, gy - 1, gy + 1, gy > 0, gy < gy_count - 1


def greet_around():
    east, west, north, south, has_north, has_south = compass()
    barrier = pltpu.get_barrier_semaphore()

    def greet(device):
        pl.semaphore_signal(
            barrier, inc=1, device_id=device, device_id_type=pl.DeviceIdType.MESH
        )

    greet({"gx": east})
    greet({"gx": west})

    @pl.when(has_north)
    def _():
        for device in ({"gy": north}, {"gy": north, "gx": east}, {"gy": north, "gx": west}):
            greet(device)

    @pl.when(has_south)
    def _():
        for device in ({"gy": south}, {"gy": south, "gx": east}, {"gy": south, "gx": west}):
            greet(device)


def wait_around():
    east, west, north, south, has_north, has_south = compass()
    peers = 2 + 3 * has_north.astype(jnp.int32) + 3 * has_south.astype(jnp.int32)
    pl.semaphore_wait(pltpu.get_barrier_semaphore(), peers)


def ring_copies(dims, ring, first_rows, last_rows, south_in, north_in, send, recv):
    rows, levels, width, variables, depth = dims
    east, west, north, south, has_north, has_south = compass()
    top, bottom = pl.ds(depth, depth), pl.ds(rows, depth)
    body, above, below = pl.ds(depth, rows), pl.ds(0, depth), pl.ds(depth + rows, depth)
    first, last = pl.ds(2 * SIDE, SIDE), pl.ds(SIDE + width, SIDE)
    before, after = pl.ds(SIDE, SIDE), pl.ds(2 * SIDE + width, SIDE)

    def copy(source, target, place, device):
        return pltpu.make_async_remote_copy(
            src_ref=source, dst_ref=target, send_sem=send.at[place], recv_sem=recv.at[place],
            device_id=device, device_id_type=pl.DeviceIdType.MESH,
        )

    across = [
        copy(ring.at[body, last], ring.at[body, before], 0, {"gx": east}),
        copy(ring.at[body, first], ring.at[body, after], 1, {"gx": west}),
    ]
    up = [
        copy(first_rows, south_in, 2, {"gy": north}),
        copy(ring.at[top, last], ring.at[below, before], 3, {"gy": north, "gx": east}),
        copy(ring.at[top, first], ring.at[below, after], 4, {"gy": north, "gx": west}),
    ]
    down = [
        copy(last_rows, north_in, 5, {"gy": south}),
        copy(ring.at[bottom, last], ring.at[above, before], 6, {"gy": south, "gx": east}),
        copy(ring.at[bottom, first], ring.at[above, after], 7, {"gy": south, "gx": west}),
    ]

    def start():
        @pl.when(has_north)
        def _():
            for item in up:
                item.start()

        @pl.when(has_south)
        def _():
            for item in down:
                item.start()

        for item in across:
            item.start()

    def wait():
        for item in across:
            item.wait_recv()
            item.wait_send()

        @pl.when(has_north)
        def _():
            for item in down:
                item.wait_recv()
            for item in up:
                item.wait_send()

        @pl.when(has_south)
        def _():
            for item in up:
                item.wait_recv()
            for item in down:
                item.wait_send()

    return start, wait


def fill_halo_rows(dims, ring, from_south, from_north):
    rows, levels, width, variables, depth = dims
    east, west, north, south, has_north, has_south = compass()
    inner, whole = pl.ds(2 * SIDE, width), pl.ds(SIDE, width + 2 * SIDE)

    @pl.when(has_south)
    def _():
        for d in range(depth):
            ring[depth + rows + d, inner] = from_south(d)

    @pl.when(jnp.logical_not(has_south))
    def _():
        for d in range(depth):
            ring[depth + rows + d, whole] = ring[depth + rows - 1 - d, whole]

    @pl.when(has_north)
    def _():
        for d in range(depth):
            ring[d, inner] = from_north(d)

    @pl.when(jnp.logical_not(has_north))
    def _():
        for d in range(depth):
            ring[d, whole] = ring[2 * depth - 1 - d, whole]


def diffuse(dims, ring, work, kap):
    rows, levels, width, variables, depth = dims
    for step in range(1, depth + 1):
        source, target = (ring, work) if step % 2 else (work, ring)
        start, stop = (SIDE, width + 3 * SIDE) if step < depth else (2 * SIDE, width + 2 * SIDE)

        @pl.loop(0, rows // 2 + depth - step)
        def _(pair, source=source, target=target, start=start, stop=stop, step=step):
            y = step + 2 * pair
            for x in range(start, stop, 6 * SIDE):
                size = min(6 * SIDE, stop - x)
                here = pl.ds(x, size)
                held = [source[y + i, here] for i in (-1, 0, 1, 2)]
                for i in (0, 1):
                    center = held[i + 1]
                    sides = source[y + i, pl.ds(x - 1, size)] + source[y + i, pl.ds(x + 1, size)]
                    change = (held[i] + held[i + 2]) + sides - 4.0 * center
                    target[y + i, here] = center + kap[y + i, here] * change


def split(value):
    high = value.astype(bf16)
    return high, (value - high.astype(f32)).astype(bf16)


def stacked_weights(weights):
    high, low = split(weights)
    return jnp.concatenate(
        [
            jnp.concatenate([high, high], axis=1),
            jnp.concatenate([low, jnp.zeros_like(low)], axis=1),
        ],
        axis=0,
    )


def mixed(weights_ref, value, axis):
    half = weights_ref.shape[0] // 2
    numbers = NT if axis else NN
    both = lax.dot_general(
        weights_ref[...], jnp.concatenate(split(value), axis=axis), numbers,
        preferred_element_type=f32,
    )
    return both[:half] + both[half:]


def lane_grid(lanes, levels):
    row = lax.broadcasted_iota(jnp.int32, (lanes, lanes), 0)
    col = lax.broadcasted_iota(jnp.int32, (lanes, lanes), 1)
    row_block, col_block = row // levels, col // levels
    return row - row_block * levels, col - col_block * levels, row_block == col_block


def vertical_blocks(bounds_ref, lanes, levels, transposed):
    row, col, same = lane_grid(lanes, levels)
    bounds = bounds_ref[...].astype(f32)
    limits = []
    for side in range(2):
        line = jnp.concatenate([bounds[side : side + 1]] * (lanes // levels), axis=1)
        spread = jnp.broadcast_to(line, (lanes, lanes))
        limits.append(spread if transposed else spread.T)
    reach = (row if transposed else col).astype(f32)
    distance = jnp.abs(row - col).astype(f32)
    inside = same & (reach >= limits[0]) & (reach <= limits[1])
    return jnp.where(inside, jnp.exp(-distance / vertical_scale), 0.0)


def static_blocks(static_ref, levels):
    variables = static_ref.shape[0]
    lanes = variables * levels
    same = lane_grid(lanes, levels)[2]
    tiles = [jnp.concatenate([static_ref[v]] * variables, axis=1) for v in range(variables)]
    return jnp.where(same, jnp.concatenate(tiles, axis=0), 0.0)


def pack_row(dims, ring, first_rows, last_rows, y, value):
    rows, levels, width, variables, depth = dims
    ring[depth + y, pl.ds(2 * SIDE, width)] = value
    if y < depth:
        first_rows[y] = value.astype(bf16)
    if y >= rows - depth:
        last_rows[y - (rows - depth)] = value.astype(bf16)


def forward_kernel(
    dims, ens_scale, bounds, static_vert, kappa, alpha_hbm, chi_hbm, perturb_hbm, out, kap,
    alpha, chi, perturb, ring, work, rows_out, rows_in, kappa_in, spread, acc, static, mix, load,
    send, recv,
):
    rows, levels, width, variables, depth = dims
    groups, lanes = ring.shape[0], ring.shape[3]
    count, column = rows * levels, variables * levels
    group_rows = lanes * rows
    greet_around()
    loads = [
        pltpu.make_async_copy(
            alpha_hbm.at[pl.ds(g * group_rows, group_rows)],
            alpha.at[pl.ds(g * group_rows, group_rows)], load.at[g],
        )
        for g in range(groups)
    ]
    load_chi = pltpu.make_async_copy(chi_hbm, chi, load.at[groups])
    load_perturb = pltpu.make_async_copy(perturb_hbm, perturb, load.at[groups + 1])
    for item in loads:
        item.start()
    load_chi.start()
    load_perturb.start()
    for y in range(rows):
        kap[depth + y, pl.ds(2 * SIDE, width)] = jnp.broadcast_to(
            kappa[y : y + 1, :], (lanes, width)
        ).T
    moves = [
        ring_copies(
            dims, ring.at[g], rows_out.at[g, 0], rows_out.at[g, 1], rows_in.at[g, 0],
            rows_in.at[g, 1], send.at[g], recv.at[g],
        )
        for g in range(groups)
    ]
    move_kappa = ring_copies(
        dims, kap, kappa.at[pl.ds(0, SIDE)], kappa.at[pl.ds(rows - SIDE, SIDE)], kappa_in.at[0],
        kappa_in.at[1], send.at[groups], recv.at[groups],
    )
    for g in range(groups):
        loads[g].wait()
        for y in range(rows):
            block = alpha[pl.ds(g * group_rows + y, lanes, stride=rows), :]
            pack_row(dims, ring.at[g], rows_out.at[g, 0], rows_out.at[g, 1], y, block.T)
        if g == 0:
            wait_around()
        moves[g][0]()
        if g == 0:
            move_kappa[0]()
    mix[...] = stacked_weights(
        static_blocks(static_vert, levels)
        * jnp.where(lax.axis_index("mem") == 0, static_weight, 0.0)
    )
    load_chi.wait()
    for y in range(rows):
        static[y] = mixed(mix, chi[pl.ds(y, column, stride=rows), :], 0)
    mix[...] = stacked_weights(vertical_blocks(bounds, lanes, levels, False))
    move_kappa[1]()
    fill_halo_rows(
        dims, kap,
        lambda d: jnp.broadcast_to(kappa_in[0, d : d + 1, :], (lanes, width)).T,
        lambda d: jnp.broadcast_to(
            kappa_in[1, SIDE - depth + d : SIDE - depth + d + 1, :], (lanes, width)
        ).T,
    )
    for g in range(groups):
        moves[g][1]()
        fill_halo_rows(
            dims, ring.at[g], lambda d: rows_in[g, 0, d].astype(f32),
            lambda d: rows_in[g, 1, d].astype(f32),
        )
        diffuse(dims, ring.at[g], work, kap)
        for y in range(rows):
            spread[pl.ds(g * group_rows + y, lanes, stride=rows), :] = mixed(
                mix, ring[g, depth + y, pl.ds(2 * SIDE, width)], 1
            )
    load_perturb.wait()
    members = perturb.shape[0]

    @pl.loop(0, levels)
    def _(level):
        place = pl.multiple_of(level * rows, rows)
        spreads = [spread[pl.ds(k * count + place, rows), :] for k in range(members)]
        for v in range(variables):
            total = perturb[0, v, pl.ds(place, rows), :].astype(f32) * spreads[0]
            for k in range(1, members):
                total = total + perturb[k, v, pl.ds(place, rows), :].astype(f32) * spreads[k]
            acc[pl.ds(v * count + place, rows), :] = total

    for y in range(rows):
        out[y] = (ens_scale * acc[pl.ds(y, column, stride=rows), :] + static[y]).T


def backward_kernel(
    dims, ens_scale, bounds, static_vert, kappa, grad, kap, alpha_hbm, chi_hbm, perturb_hbm,
    out_alpha, out_chi, alpha, chi, perturb, ring, work, rows_out, rows_in, field, nat, mix, load,
    send, recv,
):
    rows, levels, width, variables, depth = dims
    groups, lanes = ring.shape[0], ring.shape[3]
    count, column = rows * levels, variables * levels
    group_rows = lanes * rows
    group_members = lanes // levels
    inner = pl.ds(2 * SIDE, width)
    greet_around()
    loads = [
        pltpu.make_async_copy(
            perturb_hbm.at[pl.ds(g * group_members, group_members)],
            perturb.at[pl.ds(g * group_members, group_members)], load.at[g],
        )
        for g in range(groups)
    ]
    load_chi = pltpu.make_async_copy(chi_hbm, chi, load.at[groups])
    load_alpha = pltpu.make_async_copy(alpha_hbm, alpha, load.at[groups + 1])
    for item in loads:
        item.start()
    load_chi.start()
    load_alpha.start()
    for y in range(rows):
        nat[pl.ds(y, column, stride=rows), :] = ens_scale * grad[y].T
    moves = [
        ring_copies(
            dims, ring.at[g], rows_out.at[g, 0], rows_out.at[g, 1], rows_in.at[g, 0],
            rows_in.at[g, 1], send.at[g], recv.at[g],
        )
        for g in range(groups)
    ]
    for g in range(groups):
        loads[g].wait()

        @pl.loop(0, levels)
        def _(level, g=g):
            place = pl.multiple_of(level * rows, rows)
            slopes = [nat[pl.ds(v * count + place, rows), :] for v in range(variables)]
            for k in range(g * group_members, (g + 1) * group_members):
                total = perturb[k, 0, pl.ds(place, rows), :].astype(f32) * slopes[0]
                for v in range(1, variables):
                    total = total + perturb[k, v, pl.ds(place, rows), :].astype(f32) * slopes[v]
                field[pl.ds(k * count + place, rows), :] = total * kappa[...]

        for y in range(rows):
            block = field[pl.ds(g * group_rows + y, lanes, stride=rows), :]
            pack_row(dims, ring.at[g], rows_out.at[g, 0], rows_out.at[g, 1], y, block.T)
        if g == 0:
            wait_around()
        moves[g][0]()
    mix[...] = stacked_weights(static_weight * static_blocks(static_vert, levels).T)
    load_chi.wait()
    for y in range(rows):
        line = pl.ds(y, column, stride=rows)
        out_chi[line, :] = chi[line, :] + mixed(mix, grad[y], 1)
    mix[...] = stacked_weights(vertical_blocks(bounds, lanes, levels, True))
    load_alpha.wait()
    inverse = 1.0 / kappa[...]
    for g in range(groups):
        moves[g][1]()
        fill_halo_rows(
            dims, ring.at[g], lambda d: rows_in[g, 0, d].astype(f32),
            lambda d: rows_in[g, 1, d].astype(f32),
        )
        diffuse(dims, ring.at[g], work, kap)
        for y in range(rows):
            line = pl.ds(g * group_rows + y, lanes, stride=rows)
            out_alpha[line, :] = alpha[line, :] + inverse[y : y + 1] * mixed(
                mix, ring[g, depth + y, inner], 1
            )


def observe_kernel(
    rows, band, padded, count_ref, table_ref, anchor_ref, weight_ref, background_ref, observed_ref,
    inv_var_ref, jacobian_ref, out_ref, high_ref, low_ref,
):
    places = anchor_ref.shape[1]
    anchor = anchor_ref[...]
    anchor_row = anchor // band
    anchor_col = anchor - anchor_row * band
    slot = lax.broadcasted_iota(jnp.int32, (padded, places), 0)
    at_left = slot == anchor_col
    at_right = slot == anchor_col + 1
    total = background_ref[...].astype(f32).T
    for y in range(rows):
        upper = anchor_row == y
        lower = anchor_row == y - 1
        zero = jnp.zeros(anchor.shape, f32)
        left = jnp.where(upper, weight_ref[0:1], jnp.where(lower, weight_ref[2:3], zero))
        right = jnp.where(upper, weight_ref[1:2], jnp.where(lower, weight_ref[3:4], zero))
        weights = jnp.where(at_left, left, jnp.where(at_right, right, 0.0))
        high, low = split(weights)
        high_ref[y] = high
        low_ref[y] = low
        cells = table_ref[y]
        total = total + lax.dot_general(cells, high, TN, preferred_element_type=f32)
        total = total + lax.dot_general(cells, low, TN, preferred_element_type=f32)
    bent = jnp.tanh(total)
    modeled = jnp.dot(jacobian_ref[...], bent, precision=highest, preferred_element_type=f32)
    position = lax.broadcasted_iota(jnp.int32, modeled.shape, 1)
    misfit = jnp.where(
        position < count_ref[0], (modeled - observed_ref[...]) * inv_var_ref[...], 0.0
    )
    back = lax.dot_general(
        jacobian_ref[...], misfit, TN, precision=highest, preferred_element_type=f32
    )
    state_high, state_low = split((1.0 - bent * bent) * back)
    for y in range(rows):
        high = high_ref[y]
        cells = lax.dot_general(high, state_high, NT, preferred_element_type=f32)
        cells = cells + lax.dot_general(low_ref[y], state_high, NT, preferred_element_type=f32)
        cells = cells + lax.dot_general(high, state_low, NT, preferred_element_type=f32)
        out_ref[y] = cells


def choose(index, options):
    result = options[0]
    for place in range(1, len(options)):
        result = jnp.where(index == place, options[place], result)
    return result


def body(
    alpha, perturb, chi, kappa, vert_bounds, static_vert, fine_owner, obs_stencil, obs_weight,
    background, observed, inv_var, jacobian, obs_count,
):
    members, levels, rows, width = alpha.shape
    variables = perturb.shape[1]
    column = variables * levels
    depth = NDIFF
    groups = lax.axis_size("mem")
    band = width // groups
    shift = band // 2
    rim = shift + 1
    me = lax.axis_index("mem")
    count = rows * levels
    places = obs_stencil.shape[0]
    dims = (rows, levels, width, variables, depth)
    ens_scale = ensemble_weight / math.sqrt(members * groups - 1)
    owners = fine_owner[0]
    band_ids = lax.iota(jnp.int32, groups)

    def band_of(group):
        return jnp.sum(jnp.where(owners == group, band_ids, 0))

    smem = pl.BlockSpec(memory_space=pltpu.SMEM)
    vmem = pl.BlockSpec(memory_space=pltpu.VMEM)
    hbm = pl.BlockSpec(memory_space=pl.ANY)
    lanes = column
    grouped = members * levels // lanes
    ring_rows, ring_width = rows + 2 * depth, width + 4 * SIDE
    alpha_flat = alpha.reshape(members * count, width)
    chi_flat = chi.reshape(variables * count, width)
    perturb_flat = perturb.reshape(members, variables, count, width)

    def exchange_scratch(extra):
        return [
            pltpu.VMEM((grouped, 2, depth, width, lanes), bf16),
            pltpu.VMEM((grouped, 2, depth, width, lanes), bf16),
        ] + extra

    tile_scratch = [
        pltpu.VMEM((members * count, width), f32),
        pltpu.VMEM((variables * count, width), f32),
        pltpu.VMEM((members, variables, count, width), bf16),
        pltpu.VMEM((grouped, ring_rows, ring_width, lanes), f32),
        pltpu.VMEM((ring_rows, ring_width, lanes), f32),
    ]
    partial, kap = pl.pallas_call(
        lambda *refs: forward_kernel(dims, ens_scale, *refs),
        in_specs=[vmem, vmem, vmem, hbm, hbm, hbm],
        out_specs=[vmem, vmem],
        out_shape=[
            jax.ShapeDtypeStruct((rows, width, column), f32),
            jax.ShapeDtypeStruct((ring_rows, ring_width, lanes), f32),
        ],
        scratch_shapes=tile_scratch + exchange_scratch([
            pltpu.VMEM((2, SIDE, width), f32),
            pltpu.VMEM((members * count, width), f32),
            pltpu.VMEM((variables * count, width), f32),
            pltpu.VMEM((rows, column, width), f32),
            pltpu.VMEM((2 * lanes, 2 * lanes), bf16),
            pltpu.SemaphoreType.DMA((grouped + 2,)),
            pltpu.SemaphoreType.DMA((grouped + 1, 8)),
            pltpu.SemaphoreType.DMA((grouped + 1, 8)),
        ]),
        compiler_params=pltpu.CompilerParams(
            collective_id=0, has_side_effects=True, vmem_limit_bytes=40 << 20
        ),
        name="forward",
    )(vert_bounds, static_vert, kappa, alpha_flat, chi_flat, perturb_flat)

    own_band = band_of(me)
    east_rim = shifted(partial[:, :rim].astype(bf16), "gx", -1)
    near = [partial[:, b * band + shift : (b + 1) * band] for b in range(groups)]
    far = [partial[:, b * band : b * band + rim] for b in range(1, groups)]
    far.append(east_rim.astype(f32))
    halves = []
    for parts in (near, far):
        half = choose(own_band, parts)
        for hop in range(1, groups):
            away = choose(band_of((me + hop) % groups), parts).astype(bf16)
            half = half + shifted(away, "mem", hop).astype(f32)
        halves.append(half)
    increment = jnp.concatenate(halves, axis=1)
    padded = -(-(band + 1) // 16) * 16
    table = jnp.pad(increment.astype(bf16), ((0, 0), (0, padded - band - 1), (0, 0)))

    region_grad = pl.pallas_call(
        lambda *refs: observe_kernel(rows, band, padded, *refs),
        in_specs=[smem] + [vmem] * 7,
        out_specs=vmem,
        out_shape=jax.ShapeDtypeStruct((rows, padded, column), f32),
        scratch_shapes=[
            pltpu.VMEM((rows, padded, places), bf16),
            pltpu.VMEM((rows, padded, places), bf16),
        ],
        compiler_params=params(),
        name="observe",
    )(
        obs_count, table, obs_stencil.reshape(1, places), obs_weight, background, observed,
        inv_var, jacobian,
    )

    near, far = region_grad[:, : band - shift], region_grad[:, band - shift : band + 1]
    far_pieces = [(own_band, far)]
    for hop in range(1, groups):
        far_pieces.append((band_of((me - hop) % groups), shifted(far, "mem", hop)))
    rim_grad = choose_equal(groups - 1, far_pieces)
    near, rim_grad = lax.optimization_barrier((near, rim_grad))
    west_rim = shifted(rim_grad, "gx", 1)
    near_pieces = [(own_band, near)]
    for hop in range(1, groups):
        near_pieces.append((band_of((me - hop) % groups), shifted(near, "mem", hop)))
    grad_cells = jnp.pad(west_rim, ((0, 0), (0, width - rim), (0, 0)))
    for b in range(groups):
        before = b * band + shift
        grad_cells = grad_cells + jnp.pad(
            choose_equal(b, near_pieces), ((0, 0), (before, width - (b + 1) * band), (0, 0))
        )
    for b in range(1, groups):
        before = b * band
        grad_cells = grad_cells + jnp.pad(
            choose_equal(b - 1, far_pieces), ((0, 0), (before, width - before - rim), (0, 0))
        )

    grad_alpha, grad_chi = pl.pallas_call(
        lambda *refs: backward_kernel(dims, ens_scale, *refs),
        in_specs=[vmem, vmem, vmem, vmem, vmem, hbm, hbm, hbm],
        out_specs=[vmem, vmem],
        out_shape=[
            jax.ShapeDtypeStruct((members * count, width), f32),
            jax.ShapeDtypeStruct((variables * count, width), f32),
        ],
        scratch_shapes=tile_scratch + exchange_scratch([
            pltpu.VMEM((members * count, width), f32),
            pltpu.VMEM((variables * count, width), f32),
            pltpu.VMEM((2 * lanes, 2 * lanes), bf16),
            pltpu.SemaphoreType.DMA((grouped + 2,)),
            pltpu.SemaphoreType.DMA((grouped, 8)),
            pltpu.SemaphoreType.DMA((grouped, 8)),
        ]),
        compiler_params=pltpu.CompilerParams(
            collective_id=1, has_side_effects=True, vmem_limit_bytes=40 << 20
        ),
        name="backward",
    )(vert_bounds, static_vert, kappa, grad_cells, kap, alpha_flat, chi_flat, perturb_flat)
    return grad_alpha.reshape(alpha.shape), grad_chi.reshape(chi.shape)


def choose_equal(wanted, pieces):
    result = pieces[0][1]
    for index, piece in pieces[1:]:
        result = jnp.where(index == wanted, piece, result)
    return result


def solution(mesh):
    in_specs = (
        P("mem", None, "gy", "gx"),
        P("mem", None, None, "gy", "gx"),
        P(None, None, "gy", "gx"),
        P("gy", "gx"),
        P(),
        P(),
        P(("gy", "gx"), None),
        P(("mem", "gy", "gx")),
        P(None, ("mem", "gy", "gx")),
        P(("mem", "gy", "gx"), None),
        P(None, ("mem", "gy", "gx")),
        P(None, ("mem", "gy", "gx")),
        P(),
        P(("mem", "gy", "gx")),
    )
    out_specs = (P("mem", None, "gy", "gx"), P(None, None, "gy", "gx"))
    return jax.shard_map(body, mesh=mesh, in_specs=in_specs, out_specs=out_specs, check_vma=False)
```

```python
import math

import jax
import jax.numpy as jnp
from jax import lax
from jax.experimental import pallas as pl
from jax.experimental.pallas import tpu as pltpu
from jax.sharding import PartitionSpec as P

NDIFF = 4

ensemble_weight = 0.8
static_weight = 0.6
vertical_scale = 2.0
code_limit = 32767.0
f32 = jnp.float32
bf16 = jnp.bfloat16
SIDE = 8
NN = (((1,), (0,)), ((), ()))
NT = (((1,), (1,)), ((), ()))
TN = (((0,), (0,)), ((), ()))


def compass():
    gx, gy = lax.axis_index("gx"), lax.axis_index("gy")
    gx_count, gy_count = lax.axis_size("gx"), lax.axis_size("gy")
    east, west = lax.rem(gx + 1, gx_count), lax.rem(gx + gx_count - 1, gx_count)
    return east, west, gy - 1, gy + 1, gy > 0, gy < gy_count - 1


def greet_around(partners):
    east, west, north, south, has_north, has_south = compass()
    barrier = pltpu.get_barrier_semaphore()

    def greet(device):
        pl.semaphore_signal(
            barrier, inc=1, device_id=device, device_id_type=pl.DeviceIdType.MESH
        )

    for device in [{"gx": east}, {"gx": west}] + partners:
        greet(device)

    @pl.when(has_north)
    def _():
        for device in ({"gy": north}, {"gy": north, "gx": east}, {"gy": north, "gx": west}):
            greet(device)

    @pl.when(has_south)
    def _():
        for device in ({"gy": south}, {"gy": south, "gx": east}, {"gy": south, "gx": west}):
            greet(device)


def wait_around(partners):
    east, west, north, south, has_north, has_south = compass()
    peers = partners + 2 + 3 * has_north.astype(jnp.int32) + 3 * has_south.astype(jnp.int32)
    pl.semaphore_wait(pltpu.get_barrier_semaphore(), peers)


def ring_copies(dims, ring, first_rows, last_rows, south_in, north_in, send, recv):
    rows, levels, width, variables, depth = dims
    east, west, north, south, has_north, has_south = compass()
    top, bottom = pl.ds(depth, depth), pl.ds(rows, depth)
    body, above, below = pl.ds(depth, rows), pl.ds(0, depth), pl.ds(depth + rows, depth)
    first, last = pl.ds(2 * SIDE, SIDE), pl.ds(SIDE + width, SIDE)
    before, after = pl.ds(SIDE, SIDE), pl.ds(2 * SIDE + width, SIDE)

    def copy(source, target, place, device):
        return pltpu.make_async_remote_copy(
            src_ref=source, dst_ref=target, send_sem=send.at[place], recv_sem=recv.at[place],
            device_id=device, device_id_type=pl.DeviceIdType.MESH,
        )

    across = [
        copy(ring.at[body, last], ring.at[body, before], 0, {"gx": east}),
        copy(ring.at[body, first], ring.at[body, after], 1, {"gx": west}),
    ]
    up = [
        copy(first_rows, south_in, 2, {"gy": north}),
        copy(ring.at[top, last], ring.at[below, before], 3, {"gy": north, "gx": east}),
        copy(ring.at[top, first], ring.at[below, after], 4, {"gy": north, "gx": west}),
    ]
    down = [
        copy(last_rows, north_in, 5, {"gy": south}),
        copy(ring.at[bottom, last], ring.at[above, before], 6, {"gy": south, "gx": east}),
        copy(ring.at[bottom, first], ring.at[above, after], 7, {"gy": south, "gx": west}),
    ]

    def start():
        @pl.when(has_north)
        def _():
            for item in up:
                item.start()

        @pl.when(has_south)
        def _():
            for item in down:
                item.start()

        for item in across:
            item.start()

    def wait():
        for item in across:
            item.wait_recv()
            item.wait_send()

        @pl.when(has_north)
        def _():
            for item in down:
                item.wait_recv()
            for item in up:
                item.wait_send()

        @pl.when(has_south)
        def _():
            for item in up:
                item.wait_recv()
            for item in down:
                item.wait_send()

    return start, wait


def fill_halo_rows(dims, ring, from_south, from_north):
    rows, levels, width, variables, depth = dims
    east, west, north, south, has_north, has_south = compass()
    inner, whole = pl.ds(2 * SIDE, width), pl.ds(SIDE, width + 2 * SIDE)

    @pl.when(has_south)
    def _():
        for d in range(depth):
            ring[depth + rows + d, inner] = from_south(d)

    @pl.when(jnp.logical_not(has_south))
    def _():
        for d in range(depth):
            ring[depth + rows + d, whole] = ring[depth + rows - 1 - d, whole]

    @pl.when(has_north)
    def _():
        for d in range(depth):
            ring[d, inner] = from_north(d)

    @pl.when(jnp.logical_not(has_north))
    def _():
        for d in range(depth):
            ring[d, whole] = ring[2 * depth - 1 - d, whole]


def diffuse(dims, ring, work, kap):
    rows, levels, width, variables, depth = dims
    for step in range(1, depth + 1):
        source, target = (ring, work) if step % 2 else (work, ring)
        start, stop = (SIDE, width + 3 * SIDE) if step < depth else (2 * SIDE, width + 2 * SIDE)

        @pl.loop(0, rows // 2 + depth - step)
        def _(pair, source=source, target=target, start=start, stop=stop, step=step):
            y = step + 2 * pair
            for x in range(start, stop, 6 * SIDE):
                size = min(6 * SIDE, stop - x)
                here = pl.ds(x, size)
                held = [source[y + i, here] for i in (-1, 0, 1, 2)]
                for i in (0, 1):
                    center = held[i + 1]
                    sides = source[y + i, pl.ds(x - 1, size)] + source[y + i, pl.ds(x + 1, size)]
                    change = (held[i] + held[i + 2]) + sides - 4.0 * center
                    target[y + i, here] = center + kap[y + i, here] * change


def split(value):
    high = value.astype(bf16)
    return high, (value - high.astype(f32)).astype(bf16)


def stacked_weights(weights):
    high, low = split(weights)
    return jnp.concatenate(
        [
            jnp.concatenate([high, high], axis=1),
            jnp.concatenate([low, jnp.zeros_like(low)], axis=1),
        ],
        axis=0,
    )


def mixed(weights_ref, value, axis):
    half = weights_ref.shape[0] // 2
    numbers = NT if axis else NN
    both = lax.dot_general(
        weights_ref[...], jnp.concatenate(split(value), axis=axis), numbers,
        preferred_element_type=f32,
    )
    return both[:half] + both[half:]


def lane_grid(lanes, levels):
    row = lax.broadcasted_iota(jnp.int32, (lanes, lanes), 0)
    col = lax.broadcasted_iota(jnp.int32, (lanes, lanes), 1)
    row_block, col_block = row // levels, col // levels
    return row - row_block * levels, col - col_block * levels, row_block == col_block


def vertical_blocks(bounds_ref, lanes, levels, transposed):
    row, col, same = lane_grid(lanes, levels)
    bounds = bounds_ref[...].astype(f32)
    limits = []
    for side in range(2):
        line = jnp.concatenate([bounds[side : side + 1]] * (lanes // levels), axis=1)
        spread = jnp.broadcast_to(line, (lanes, lanes))
        limits.append(spread if transposed else spread.T)
    reach = (row if transposed else col).astype(f32)
    distance = jnp.abs(row - col).astype(f32)
    inside = same & (reach >= limits[0]) & (reach <= limits[1])
    return jnp.where(inside, jnp.exp(-distance / vertical_scale), 0.0)


def static_blocks(static_ref, levels):
    variables = static_ref.shape[0]
    lanes = variables * levels
    same = lane_grid(lanes, levels)[2]
    tiles = [jnp.concatenate([static_ref[v]] * variables, axis=1) for v in range(variables)]
    return jnp.where(same, jnp.concatenate(tiles, axis=0), 0.0)


def pack_row(dims, ring, first_rows, last_rows, y, value):
    rows, levels, width, variables, depth = dims
    ring[depth + y, pl.ds(2 * SIDE, width)] = value
    if y < depth:
        first_rows[y] = value.astype(bf16)
    if y >= rows - depth:
        last_rows[y - (rows - depth)] = value.astype(bf16)


def band_selector(owner, groups):
    def band_of(group):
        result = 0
        for b in range(groups):
            result = result + jnp.where(owner[0, b] == group, b, 0)
        return result

    return band_of


def choose(index, options):
    result = options[0]
    for place in range(1, len(options)):
        result = jnp.where(index == place, options[place], result)
    return result


def coded(value):
    largest = jnp.maximum(jnp.max(jnp.abs(value), axis=0, keepdims=True), 1e-30)
    codes = jnp.round(value * (code_limit / largest)).astype(jnp.int16)
    return codes, jnp.broadcast_to(largest * (1.0 / code_limit), (SIDE, value.shape[1]))


def step_kernel(
    dims, ens_scale, owner, count, bounds, static_vert, kappa, jacobian_ref, anchor_hbm, weight_hbm,
    background_hbm, observed_hbm, inv_var_hbm, alpha_hbm, chi_hbm, perturb_hbm, out_alpha, out_chi,
    alpha, chi, perturb, anchor_ref, weight_ref, background_ref, observed_ref, inv_var_ref, kap,
    ring, back_ring, work, rows_out, rows_in, back_rows_out, back_rows_in, kappa_in, field, nat,
    static, mix, partial, high, low, table, base, rim_out, rim_in, near_out, near_in, far_out,
    far_in, near_code, near_scale, far_code, far_scale, near_codes, near_scales, far_codes,
    far_scales, turn_out, turn_scale, turn_in, turn_scale_in, grad, load, send, recv, ring_send,
    ring_recv,
):
    rows, levels, width, variables, depth = dims
    groups, lanes = ring.shape[0], ring.shape[3]
    cell_count, column = rows * levels, variables * levels
    group_rows, group_members = lanes * rows, lanes // levels
    members = perturb.shape[0]
    inner = pl.ds(2 * SIDE, width)
    split_count = lax.axis_size("mem")
    me, gx, gx_count = lax.axis_index("mem"), lax.axis_index("gx"), lax.axis_size("gx")
    east, west = {"gx": lax.rem(gx + 1, gx_count)}, {"gx": lax.rem(gx + gx_count - 1, gx_count)}
    hops = range(1, split_count)
    partners = [{"mem": lax.rem(me + hop, split_count)} for hop in hops]
    band = width // split_count
    shift = band // 2
    block = rows * shift
    places = anchor_ref.shape[1]

    greet_around(partners)
    group_part = [pl.ds(g * group_rows, group_rows) for g in range(groups)]
    loads = [
        pltpu.make_async_copy(alpha_hbm.at[part], alpha.at[part], load.at[g])
        for g, part in enumerate(group_part)
    ]
    others = [
        pltpu.make_async_copy(source, target, load.at[groups + i])
        for i, (source, target) in enumerate(
            [
                (chi_hbm, chi), (perturb_hbm, perturb), (anchor_hbm, anchor_ref),
                (weight_hbm, weight_ref), (background_hbm, background_ref),
                (observed_hbm, observed_ref), (inv_var_hbm, inv_var_ref),
            ]
        )
    ]
    for item in loads + others:
        item.start()

    def ring_moves(target, out_rows, in_rows, first):
        return [
            ring_copies(
                dims, target.at[g], out_rows.at[g, 0], out_rows.at[g, 1], in_rows.at[g, 0],
                in_rows.at[g, 1], ring_send.at[first + g], ring_recv.at[first + g],
            )
            for g in range(groups)
        ]

    moves = ring_moves(ring, rows_out, rows_in, 0)
    back_moves = ring_moves(back_ring, back_rows_out, back_rows_in, groups)
    move_kappa = ring_copies(
        dims, kap, kappa.at[pl.ds(0, SIDE)], kappa.at[pl.ds(rows - SIDE, SIDE)], kappa_in.at[0],
        kappa_in.at[1], ring_send.at[2 * groups], ring_recv.at[2 * groups],
    )

    def pack_group(g, source, target, out_rows):
        for y in range(rows):
            held = source[pl.ds(g * group_rows + y, lanes, stride=rows), :]
            pack_row(dims, target.at[g], out_rows.at[g, 0], out_rows.at[g, 1], y, held.T)

    for g in range(groups):
        loads[g].wait()
        pack_group(g, alpha, ring, rows_out)
        if g == 0:
            wait_around(len(partners))
        moves[g][0]()
        if g == 0:
            for y in range(rows):
                kap[depth + y, inner] = jnp.broadcast_to(kappa[y : y + 1, :], (lanes, width)).T
            move_kappa[0]()
    mix[...] = stacked_weights(
        static_blocks(static_vert, levels) * jnp.where(me == 0, static_weight, 0.0)
    )
    others[0].wait()
    for y in range(0, rows, 2):
        pair = [chi[pl.ds(y + i, column, stride=rows), :] for i in (0, 1)]
        both = mixed(mix, jnp.concatenate(pair, axis=1), 0)
        static[y], static[y + 1] = both[:, :width], both[:, width:]

    mix[...] = stacked_weights(vertical_blocks(bounds, lanes, levels, False))
    for item in others[2:]:
        item.wait()
    base[...] = background_ref[...].astype(f32).T

    @pl.loop(0, places // lanes)
    def _(chunk):
        here = pl.ds(pl.multiple_of(chunk * lanes, lanes), lanes)
        anchor = anchor_ref[:, here]
        anchor_row = anchor // band
        anchor_col = anchor - anchor_row * band
        weight = [weight_ref[q : q + 1, here] for q in range(4)]
        slot = lax.broadcasted_iota(jnp.int32, (band, lanes), 0)
        at_left, at_right = slot == anchor_col, slot == anchor_col + 1
        parts = [
            split(
                jnp.where(
                    at_left, weight[2 * d], jnp.where(at_right, weight[2 * d + 1], 0.0)
                )
            )
            for d in range(2)
        ]
        spread_row = jnp.broadcast_to(anchor_row, (shift, lanes))
        for y in range(rows):
            upper = jnp.where(spread_row == y, 1.0, 0.0).astype(bf16)
            lower = jnp.where(spread_row == y - 1, 1.0, 0.0).astype(bf16)
            for half in range(2):
                cut = slice(half * shift, (half + 1) * shift)
                place = pl.ds(half * block + y * shift, shift)
                for ref, term in ((high, 0), (low, 1)):
                    ref[place, here] = parts[0][term][cut] * upper + parts[1][term][cut] * lower
        line = lax.broadcasted_iota(jnp.int32, (rows, lanes), 0)
        past = anchor_col == band - 1
        ends = jnp.where(
            past & (line == anchor_row), weight[1],
            jnp.where(past & (line == anchor_row + 1), weight[3], 0.0),
        )
        final = pl.ds(2 * block, rows)
        high[final, here], low[final, here] = split(ends)

    move_kappa[1]()
    fill_halo_rows(
        dims, kap,
        lambda d: jnp.broadcast_to(kappa_in[0, d : d + 1, :], (lanes, width)).T,
        lambda d: jnp.broadcast_to(
            kappa_in[1, SIDE - depth + d : SIDE - depth + d + 1, :], (lanes, width)
        ).T,
    )

    def diffused(g, source, in_rows, copies):
        copies[g][1]()
        fill_halo_rows(
            dims, source.at[g], lambda d: in_rows[g, 0, d].astype(f32),
            lambda d: in_rows[g, 1, d].astype(f32),
        )
        diffuse(dims, source.at[g], work, kap)
        for y in range(0, rows, 2):
            pair = [source[g, depth + y + i, inner] for i in (0, 1)]
            both = mixed(mix, jnp.concatenate(pair, axis=0), 1)
            for i in (0, 1):
                yield y + i, pl.ds(g * group_rows + y + i, lanes, stride=rows), both[
                    :, i * width : (i + 1) * width
                ]

    for g in range(groups):
        for y, line, value in diffused(g, ring, rows_in, moves):
            field[line, :] = value
    others[1].wait()

    @pl.loop(0, levels)
    def _(level):
        place = pl.multiple_of(level * rows, rows)
        spreads = [field[pl.ds(k * cell_count + place, rows), :] for k in range(members)]
        for v in range(variables):
            total = perturb[0, v, pl.ds(place, rows), :].astype(f32) * spreads[0]
            for k in range(1, members):
                total = total + perturb[k, v, pl.ds(place, rows), :].astype(f32) * spreads[k]
            nat[pl.ds(v * cell_count + place, rows), :] = total

    for y in range(rows):
        partial[y] = (ens_scale * nat[pl.ds(y, column, stride=rows), :] + static[y]).T

    def copy(source, target, kind, hop, device):
        return pltpu.make_async_remote_copy(
            src_ref=source, dst_ref=target, send_sem=send.at[kind, hop],
            recv_sem=recv.at[kind, hop], device_id=device, device_id_type=pl.DeviceIdType.MESH,
        )

    def to_partners(source, target, kind, each):
        return [
            copy(source.at[h - 1] if each else source, target.at[h - 1], kind, h, partners[h - 1])
            for h in hops
        ]

    move_rim = copy(rim_out, rim_in, 0, 0, west)
    move_near = to_partners(near_out, near_in, 1, True)
    move_far = to_partners(far_out, far_in, 2, True)
    move_turn = [
        copy(turn_out, turn_in, 1, 0, east), copy(turn_scale, turn_scale_in, 2, 0, east)
    ]
    back_far = to_partners(far_code, far_codes, 3, False)
    back_far += to_partners(far_scale, far_scales, 4, False)
    back_near = to_partners(near_code, near_codes, 5, False)
    back_near += to_partners(near_scale, near_scales, 6, False)

    band_of = band_selector(owner, split_count)
    away = [band_of(lax.rem(me + hop, split_count)) for hop in hops]
    own_band = band_of(me)

    def columns(start):
        return jnp.concatenate([partial[y, pl.ds(start, shift), :] for y in range(rows)], axis=0)

    def edge(start):
        return jnp.concatenate([partial[y, pl.ds(start, 1), :] for y in range(rows)], axis=0)

    def near_of(index):
        return choose(index, [columns(b * band + shift) for b in range(split_count)])

    def far_of(index):
        options = [
            jnp.concatenate([columns(b * band), edge(b * band + shift)], axis=0)
            for b in range(1, split_count)
        ]
        return choose(index, options + [rim_in[...].astype(f32)])

    rim_out[...] = jnp.concatenate([columns(0), edge(shift)], axis=0).astype(bf16)
    move_rim.start()
    for h in hops:
        near_out[h - 1] = near_of(away[h - 1]).astype(bf16)
        move_near[h - 1].start()
    move_rim.wait_recv()
    for h in hops:
        far_out[h - 1] = far_of(away[h - 1]).astype(bf16)
        move_far[h - 1].start()
    near, far = near_of(own_band), far_of(own_band)
    for h in hops:
        move_near[h - 1].wait_recv()
        near = near + near_in[h - 1].astype(f32)
    table[pl.ds(0, block), :] = near.astype(bf16)
    for h in hops:
        move_far[h - 1].wait_recv()
        far = far + far_in[h - 1].astype(f32)
    table[pl.ds(block, block + rows), :] = far.astype(bf16)

    cells = table[...]
    total = base[...] + lax.dot_general(cells, high[...], TN, preferred_element_type=f32)
    total = total + lax.dot_general(cells, low[...], TN, preferred_element_type=f32)
    bent = jnp.tanh(total)
    jacobian = jacobian_ref[...]
    channels = jacobian.shape[0]
    modeled = lax.dot_general(
        stacked_weights(jacobian), jnp.concatenate(split(bent), axis=0), NN,
        preferred_element_type=f32,
    )
    modeled = modeled[:channels] + modeled[channels:]
    position = lax.broadcasted_iota(jnp.int32, modeled.shape, 1)
    misfit = jnp.where(
        position < count[0], (modeled - observed_ref[...]) * inv_var_ref[...], 0.0
    )
    misfit_high = misfit.astype(bf16).astype(f32)
    jacobian_high = jacobian.astype(bf16).astype(f32)
    back = lax.dot_general(
        jnp.concatenate(
            [jacobian_high, jacobian_high, jacobian - jacobian_high, jnp.zeros_like(jacobian)],
            axis=0,
        ).astype(bf16),
        jnp.concatenate(
            [misfit_high, misfit - misfit_high, misfit_high, jnp.zeros_like(misfit)], axis=0
        ).astype(bf16),
        TN, preferred_element_type=f32,
    )
    state_high, state_low = split((1.0 - bent * bent) * back)
    states = jnp.concatenate([state_high, state_low], axis=0)

    def cells_of(start, size):
        here = pl.ds(start, size)
        both = lax.dot_general(high[here, :], states, NT, preferred_element_type=f32)
        rest = lax.dot_general(low[here, :], state_high, NT, preferred_element_type=f32)
        return both[:, :column] + both[:, column:] + rest

    far_code[...], far_scale[...] = coded(cells_of(block, block + rows))
    for item in back_far:
        item.start()
    near_code[...], near_scale[...] = coded(cells_of(0, block))
    for item in back_near:
        item.start()

    def hop_of(index):
        gap = me - owner[0, index]
        return jnp.where(gap < 0, gap + split_count, gap)

    def fars(index, scales):
        own, rest = (far_scale, far_scales) if scales else (far_code, far_codes)
        values = [own[...]] + [rest[h - 1] for h in hops]
        return choose(hop_of(index), values if scales else [v.astype(jnp.int32) for v in values])

    for item in back_far:
        item.wait_recv()
    turn_out[...] = fars(split_count - 1, False).astype(jnp.int16)
    turn_scale[...] = fars(split_count - 1, True)
    for item in move_turn:
        item.start()
    mix[...] = stacked_weights(static_weight * static_blocks(static_vert, levels).T)
    ends = []
    for b in range(split_count - 1):
        value = fars(b, False).astype(f32) * fars(b, True)[:1]
        for y in range(rows):
            grad[y, pl.ds((b + 1) * band, shift), :] = value[y * shift : (y + 1) * shift]
        ends.append(value[block:])
    for item in back_near:
        item.wait_recv()
    nears = [near_code[...]] + [near_codes[h - 1] for h in hops]
    nears = [v.astype(jnp.int32) for v in nears]
    near_steps = [near_scale[...]] + [near_scales[h - 1] for h in hops]
    for b in range(split_count):
        value = choose(hop_of(b), nears).astype(f32) * choose(hop_of(b), near_steps)[:1]
        for y in range(rows):
            grad[y, pl.ds(b * band + shift, shift), :] = value[y * shift : (y + 1) * shift]
    for item in move_turn:
        item.wait_recv()
    turned = turn_in[...].astype(f32) * turn_scale_in[:1]
    for y in range(rows):
        grad[y, pl.ds(0, shift), :] = turned[y * shift : (y + 1) * shift]
    for b, value in enumerate([turned[block:]] + ends):
        place = pl.ds(b * band + shift, 1)
        for y in range(rows):
            grad[y, place, :] = grad[y, place, :] + value[y : y + 1]

    for y in range(rows):
        nat[pl.ds(y, column, stride=rows), :] = ens_scale * grad[y].T
    for g in range(groups):

        @pl.loop(0, levels)
        def _(level, g=g):
            place = pl.multiple_of(level * rows, rows)
            slopes = [nat[pl.ds(v * cell_count + place, rows), :] for v in range(variables)]
            for k in range(g * group_members, (g + 1) * group_members):
                total = perturb[k, 0, pl.ds(place, rows), :].astype(f32) * slopes[0]
                for v in range(1, variables):
                    total = total + perturb[k, v, pl.ds(place, rows), :].astype(f32) * slopes[v]
                field[pl.ds(k * cell_count + place, rows), :] = total * kappa[...]

        pack_group(g, field, back_ring, back_rows_out)
        back_moves[g][0]()
    for y in range(0, rows, 2):
        both = mixed(mix, jnp.concatenate([grad[y], grad[y + 1]], axis=0), 1)
        for i in (0, 1):
            line = pl.ds(y + i, column, stride=rows)
            out_chi[line, :] = chi[line, :] + both[:, i * width : (i + 1) * width]
    mix[...] = stacked_weights(vertical_blocks(bounds, lanes, levels, True))
    inverse = 1.0 / kappa[...]
    for g in range(groups):
        for y, line, value in diffused(g, back_ring, back_rows_in, back_moves):
            out_alpha[line, :] = alpha[line, :] + inverse[y : y + 1] * value
    for item in [move_rim] + move_turn + move_near + move_far + back_near + back_far:
        item.wait_send()


def body(
    alpha, perturb, chi, kappa, vert_bounds, static_vert, fine_owner, obs_stencil, obs_weight,
    background, observed, inv_var, jacobian, obs_count,
):
    members, levels, rows, width = alpha.shape
    variables = perturb.shape[1]
    column = variables * levels
    depth = NDIFF
    count = rows * levels
    dims = (rows, levels, width, variables, depth)
    ens_scale = ensemble_weight / math.sqrt(members * lax.axis_size("mem") - 1)
    split_count = lax.axis_size("mem")
    places = obs_stencil.shape[0]
    shift = width // split_count // 2
    block = rows * shift
    grouped = members * levels // column
    ring_shape = (rows + 2 * depth, width + 4 * SIDE, column)
    smem = pl.BlockSpec(memory_space=pltpu.SMEM)
    vmem = pl.BlockSpec(memory_space=pltpu.VMEM)
    hbm = pl.BlockSpec(memory_space=pltpu.HBM)
    rings = pltpu.VMEM((grouped,) + ring_shape, f32)
    row_pairs = pltpu.VMEM((grouped, 2, depth, width, column), bf16)
    alpha_tile = pltpu.VMEM((members * count, width), f32)
    chi_tile = pltpu.VMEM((variables * count, width), f32)
    near, far = (block, column), (block + rows, column)
    scale = (SIDE, column)
    away = (split_count - 1,)
    i16 = jnp.int16
    grad_alpha, grad_chi = pl.pallas_call(
        lambda *refs: step_kernel(dims, ens_scale, *refs),
        in_specs=[smem, smem] + [vmem] * 4 + [hbm] * 8,
        out_specs=[vmem, vmem],
        out_shape=[
            jax.ShapeDtypeStruct((members * count, width), f32),
            jax.ShapeDtypeStruct((variables * count, width), f32),
        ],
        scratch_shapes=[
            alpha_tile,
            chi_tile,
            pltpu.VMEM((members, variables, count, width), bf16),
            pltpu.VMEM((1, places), jnp.int32),
            pltpu.VMEM((4, places), f32),
            pltpu.VMEM((places, column), bf16),
            pltpu.VMEM(observed.shape, f32),
            pltpu.VMEM(inv_var.shape, f32),
            pltpu.VMEM(ring_shape, f32),
            rings,
            rings,
            pltpu.VMEM(ring_shape, f32),
            row_pairs,
            row_pairs,
            row_pairs,
            row_pairs,
            pltpu.VMEM((2, SIDE, width), f32),
            alpha_tile,
            chi_tile,
            pltpu.VMEM((rows, column, width), f32),
            pltpu.VMEM((2 * column, 2 * column), bf16),
            pltpu.VMEM((rows, width, column), f32),
            pltpu.VMEM((2 * block + rows, places), bf16),
            pltpu.VMEM((2 * block + rows, places), bf16),
            pltpu.VMEM((2 * block + rows, column), bf16),
            pltpu.VMEM((column, places), f32),
            pltpu.VMEM(far, bf16),
            pltpu.VMEM(far, bf16),
            pltpu.VMEM(away + near, bf16),
            pltpu.VMEM(away + near, bf16),
            pltpu.VMEM(away + far, bf16),
            pltpu.VMEM(away + far, bf16),
            pltpu.VMEM(near, i16),
            pltpu.VMEM(scale, f32),
            pltpu.VMEM(far, i16),
            pltpu.VMEM(scale, f32),
            pltpu.VMEM(away + near, i16),
            pltpu.VMEM(away + scale, f32),
            pltpu.VMEM(away + far, i16),
            pltpu.VMEM(away + scale, f32),
            pltpu.VMEM(far, i16),
            pltpu.VMEM(scale, f32),
            pltpu.VMEM(far, i16),
            pltpu.VMEM(scale, f32),
            pltpu.VMEM((rows, width, column), f32),
            pltpu.SemaphoreType.DMA((grouped + 7,)),
            pltpu.SemaphoreType.DMA((7, split_count)),
            pltpu.SemaphoreType.DMA((7, split_count)),
            pltpu.SemaphoreType.DMA((2 * grouped + 1, 8)),
            pltpu.SemaphoreType.DMA((2 * grouped + 1, 8)),
        ],
        compiler_params=pltpu.CompilerParams(
            collective_id=0, has_side_effects=True, vmem_limit_bytes=60 << 20
        ),
        name="step",
    )(
        fine_owner, obs_count, vert_bounds, static_vert, kappa, jacobian,
        obs_stencil.reshape(1, places), obs_weight, background, observed, inv_var,
        alpha.reshape(members * count, width), chi.reshape(variables * count, width),
        perturb.reshape(members, variables, count, width),
    )
    return grad_alpha.reshape(alpha.shape), grad_chi.reshape(chi.shape)


def solution(mesh):
    in_specs = (
        P("mem", None, "gy", "gx"),
        P("mem", None, None, "gy", "gx"),
        P(None, None, "gy", "gx"),
        P("gy", "gx"),
        P(),
        P(),
        P(("gy", "gx"), None),
        P(("mem", "gy", "gx")),
        P(None, ("mem", "gy", "gx")),
        P(("mem", "gy", "gx"), None),
        P(None, ("mem", "gy", "gx")),
        P(None, ("mem", "gy", "gx")),
        P(),
        P(("mem", "gy", "gx")),
    )
    out_specs = (P("mem", None, "gy", "gx"), P(None, None, "gy", "gx"))
    return jax.shard_map(body, mesh=mesh, in_specs=in_specs, out_specs=out_specs, check_vma=False)
```

```python
import math

import jax
import jax.numpy as jnp
from jax import lax
from jax.experimental import pallas as pl
from jax.experimental.pallas import tpu as pltpu
from jax.sharding import PartitionSpec as P

NDIFF = 4

ensemble_weight = 0.8
static_weight = 0.6
vertical_scale = 2.0
code_limit = 32767.0
f32 = jnp.float32
bf16 = jnp.bfloat16
SIDE = 8
NN = (((1,), (0,)), ((), ()))
NT = (((1,), (1,)), ((), ()))
TN = (((0,), (0,)), ((), ()))


def compass():
    gx, gy = lax.axis_index("gx"), lax.axis_index("gy")
    gx_count, gy_count = lax.axis_size("gx"), lax.axis_size("gy")
    east, west = lax.rem(gx + 1, gx_count), lax.rem(gx + gx_count - 1, gx_count)
    return east, west, gy - 1, gy + 1, gy > 0, gy < gy_count - 1


def greet_around(partners):
    east, west, north, south, has_north, has_south = compass()
    barrier = pltpu.get_barrier_semaphore()

    def greet(device):
        pl.semaphore_signal(
            barrier, inc=1, device_id=device, device_id_type=pl.DeviceIdType.MESH
        )

    for device in [{"gx": east}, {"gx": west}] + partners:
        greet(device)

    @pl.when(has_north)
    def _():
        for device in ({"gy": north}, {"gy": north, "gx": east}, {"gy": north, "gx": west}):
            greet(device)

    @pl.when(has_south)
    def _():
        for device in ({"gy": south}, {"gy": south, "gx": east}, {"gy": south, "gx": west}):
            greet(device)


def wait_around(partners):
    east, west, north, south, has_north, has_south = compass()
    peers = partners + 2 + 3 * has_north.astype(jnp.int32) + 3 * has_south.astype(jnp.int32)
    pl.semaphore_wait(pltpu.get_barrier_semaphore(), peers)


def ring_copies(dims, ring, first_rows, last_rows, south_in, north_in, send, recv):
    rows, levels, width, variables, depth = dims
    east, west, north, south, has_north, has_south = compass()
    top, bottom = pl.ds(depth, depth), pl.ds(rows, depth)
    body, above, below = pl.ds(depth, rows), pl.ds(0, depth), pl.ds(depth + rows, depth)
    first, last = pl.ds(2 * SIDE, SIDE), pl.ds(SIDE + width, SIDE)
    before, after = pl.ds(SIDE, SIDE), pl.ds(2 * SIDE + width, SIDE)

    def copy(source, target, place, device):
        return pltpu.make_async_remote_copy(
            src_ref=source, dst_ref=target, send_sem=send.at[place], recv_sem=recv.at[place],
            device_id=device, device_id_type=pl.DeviceIdType.MESH,
        )

    across = [
        copy(ring.at[body, last], ring.at[body, before], 0, {"gx": east}),
        copy(ring.at[body, first], ring.at[body, after], 1, {"gx": west}),
    ]
    up = [
        copy(first_rows, south_in, 2, {"gy": north}),
        copy(ring.at[top, last], ring.at[below, before], 3, {"gy": north, "gx": east}),
        copy(ring.at[top, first], ring.at[below, after], 4, {"gy": north, "gx": west}),
    ]
    down = [
        copy(last_rows, north_in, 5, {"gy": south}),
        copy(ring.at[bottom, last], ring.at[above, before], 6, {"gy": south, "gx": east}),
        copy(ring.at[bottom, first], ring.at[above, after], 7, {"gy": south, "gx": west}),
    ]

    def start():
        @pl.when(has_north)
        def _():
            for item in up:
                item.start()

        @pl.when(has_south)
        def _():
            for item in down:
                item.start()

        for item in across:
            item.start()

    def wait():
        for item in across:
            item.wait_recv()
            item.wait_send()

        @pl.when(has_north)
        def _():
            for item in down:
                item.wait_recv()
            for item in up:
                item.wait_send()

        @pl.when(has_south)
        def _():
            for item in up:
                item.wait_recv()
            for item in down:
                item.wait_send()

    return start, wait


def fill_halo_rows(dims, ring, from_south, from_north):
    rows, levels, width, variables, depth = dims
    east, west, north, south, has_north, has_south = compass()
    inner, whole = pl.ds(2 * SIDE, width), pl.ds(SIDE, width + 2 * SIDE)

    @pl.when(has_south)
    def _():
        for d in range(depth):
            ring[depth + rows + d, inner] = from_south(d)

    @pl.when(jnp.logical_not(has_south))
    def _():
        for d in range(depth):
            ring[depth + rows + d, whole] = ring[depth + rows - 1 - d, whole]

    @pl.when(has_north)
    def _():
        for d in range(depth):
            ring[d, inner] = from_north(d)

    @pl.when(jnp.logical_not(has_north))
    def _():
        for d in range(depth):
            ring[d, whole] = ring[2 * depth - 1 - d, whole]


def diffuse(dims, ring, work, kap):
    rows, levels, width, variables, depth = dims
    for step in range(1, depth + 1):
        source, target = (ring, work) if step % 2 else (work, ring)
        start, stop = (SIDE, width + 3 * SIDE) if step < depth else (2 * SIDE, width + 2 * SIDE)

        @pl.loop(0, rows // 2 + depth - step)
        def _(pair, source=source, target=target, start=start, stop=stop, step=step):
            y = step + 2 * pair
            for x in range(start, stop, 6 * SIDE):
                size = min(6 * SIDE, stop - x)
                here = pl.ds(x, size)
                held = [source[y + i, here] for i in (-1, 0, 1, 2)]
                for i in (0, 1):
                    center = held[i + 1]
                    sides = source[y + i, pl.ds(x - 1, size)] + source[y + i, pl.ds(x + 1, size)]
                    change = (held[i] + held[i + 2]) + sides - 4.0 * center
                    target[y + i, here] = center + kap[y + i, here] * change


def split(value):
    high = value.astype(bf16)
    return high, (value - high.astype(f32)).astype(bf16)


def stacked_weights(weights):
    high, low = split(weights)
    return jnp.concatenate(
        [
            jnp.concatenate([high, high], axis=1),
            jnp.concatenate([low, jnp.zeros_like(low)], axis=1),
        ],
        axis=0,
    )


def mixed(weights_ref, value, axis):
    half = weights_ref.shape[0] // 2
    numbers = NT if axis else NN
    both = lax.dot_general(
        weights_ref[...], jnp.concatenate(split(value), axis=axis), numbers,
        preferred_element_type=f32,
    )
    return both[:half] + both[half:]


def lane_grid(lanes, levels):
    row = lax.broadcasted_iota(jnp.int32, (lanes, lanes), 0)
    col = lax.broadcasted_iota(jnp.int32, (lanes, lanes), 1)
    row_block, col_block = row // levels, col // levels
    return row - row_block * levels, col - col_block * levels, row_block == col_block


def vertical_blocks(bounds_ref, lanes, levels, transposed):
    row, col, same = lane_grid(lanes, levels)
    bounds = bounds_ref[...].astype(f32)
    limits = []
    for side in range(2):
        line = jnp.concatenate([bounds[side : side + 1]] * (lanes // levels), axis=1)
        spread = jnp.broadcast_to(line, (lanes, lanes))
        limits.append(spread if transposed else spread.T)
    reach = (row if transposed else col).astype(f32)
    distance = jnp.abs(row - col).astype(f32)
    inside = same & (reach >= limits[0]) & (reach <= limits[1])
    return jnp.where(inside, jnp.exp(-distance / vertical_scale), 0.0)


def static_blocks(static_ref, levels):
    variables = static_ref.shape[0]
    lanes = variables * levels
    same = lane_grid(lanes, levels)[2]
    tiles = [jnp.concatenate([static_ref[v]] * variables, axis=1) for v in range(variables)]
    return jnp.where(same, jnp.concatenate(tiles, axis=0), 0.0)


def pack_row(dims, ring, first_rows, last_rows, y, value):
    rows, levels, width, variables, depth = dims
    ring[depth + y, pl.ds(2 * SIDE, width)] = value
    if y < depth:
        first_rows[y] = value.astype(bf16)
    if y >= rows - depth:
        last_rows[y - (rows - depth)] = value.astype(bf16)


def band_selector(owner, groups):
    def band_of(group):
        result = 0
        for b in range(groups):
            result = result + jnp.where(owner[0, b] == group, b, 0)
        return result

    return band_of


def choose(index, options):
    result = options[0]
    for place in range(1, len(options)):
        result = jnp.where(index == place, options[place], result)
    return result


def coded(value):
    largest = jnp.maximum(jnp.max(jnp.abs(value), axis=0, keepdims=True), 1e-30)
    codes = jnp.round(value * (code_limit / largest)).astype(jnp.int16)
    return codes, jnp.broadcast_to(largest * (1.0 / code_limit), (SIDE, value.shape[1]))


def unpack_kernel(alpha_rows, chi_rows, out_alpha, out_chi, done):
    rows = alpha_rows.shape[0]
    moves = []
    for i, (source, target) in enumerate([(alpha_rows, out_alpha), (chi_rows, out_chi)]):
        moves += [
            pltpu.make_async_copy(source.at[y], target.at[:, y, :], done.at[i, y])
            for y in range(rows)
        ]
    for item in moves:
        item.start()
    for item in moves:
        item.wait()


def step_kernel(
    dims, ens_scale, owner, count, alpha_hbm, chi_hbm, perturb_hbm, kappa_hbm, static_hbm,
    bounds_hbm, jacobian_hbm, anchor_hbm, weight_hbm, background_hbm, observed_hbm, inv_var_hbm,
    out_alpha, out_chi, alpha, chi, perturb, kappa, static_vert, bounds, jacobian_ref, anchor_ref,
    weight_ref, background_ref, observed_ref, inv_var_ref, kap,
    ring, back_ring, work, rows_out, rows_in, back_rows_out, back_rows_in, kappa_in, field, nat,
    static, mix, partial, high, low, table, base, rim_out, rim_in, near_out, near_in, far_out,
    far_in, near_code, near_scale, far_code, far_scale, near_codes, near_scales, far_codes,
    far_scales, turn_out, turn_scale, turn_in, turn_scale_in, grad, load, send, recv, ring_send,
    ring_recv,
):
    rows, levels, width, variables, depth = dims
    groups, lanes = ring.shape[0], ring.shape[3]
    column = variables * levels
    group_members = lanes // levels
    pitch = rows + SIDE // 2
    members = perturb.shape[0]
    inner = pl.ds(2 * SIDE, width)
    split_count = lax.axis_size("mem")
    me, gx, gx_count = lax.axis_index("mem"), lax.axis_index("gx"), lax.axis_size("gx")
    east, west = {"gx": lax.rem(gx + 1, gx_count)}, {"gx": lax.rem(gx + gx_count - 1, gx_count)}
    hops = range(1, split_count)
    partners = [{"mem": lax.rem(me + hop, split_count)} for hop in hops]
    band = width // split_count
    shift = band // 2
    block = rows * shift
    places = anchor_ref.shape[1]

    greet_around(partners)
    load_alpha = [
        [
            pltpu.make_async_copy(
                alpha_hbm.at[pl.ds(g * lanes, lanes), y, :],
                alpha.at[y, pl.ds(g * lanes, lanes), :], load.at[g * rows + y],
            )
            for y in range(rows)
        ]
        for g in range(groups)
    ]
    used = groups * rows
    load_chi = [
        pltpu.make_async_copy(chi_hbm.at[:, y, :], chi.at[y], load.at[used + y])
        for y in range(rows)
    ]
    used += rows
    pairs = [
        (kappa_hbm, kappa), (static_hbm, static_vert), (bounds_hbm, bounds),
        (jacobian_hbm, jacobian_ref), (anchor_hbm, anchor_ref), (weight_hbm, weight_ref),
        (background_hbm, background_ref), (observed_hbm, observed_ref), (inv_var_hbm, inv_var_ref),
        (perturb_hbm, perturb),
    ]
    others = [
        pltpu.make_async_copy(source, target, load.at[used + i])
        for i, (source, target) in enumerate(pairs)
    ]
    for item in load_alpha[0] + others[:1]:
        item.start()
    for part in load_alpha[1:] + [load_chi, others[1:]]:
        for item in part:
            item.start()

    def ring_moves(target, out_rows, in_rows, first):
        return [
            ring_copies(
                dims, target.at[g], out_rows.at[g, 0], out_rows.at[g, 1], in_rows.at[g, 0],
                in_rows.at[g, 1], ring_send.at[first + g], ring_recv.at[first + g],
            )
            for g in range(groups)
        ]

    moves = ring_moves(ring, rows_out, rows_in, 0)
    back_moves = ring_moves(back_ring, back_rows_out, back_rows_in, groups)
    move_kappa = ring_copies(
        dims, kap, kappa.at[pl.ds(0, SIDE)], kappa.at[pl.ds(rows - SIDE, SIDE)], kappa_in.at[0],
        kappa_in.at[1], ring_send.at[2 * groups], ring_recv.at[2 * groups],
    )

    def pack_group(g, held_row, target, out_rows):
        for y in range(rows):
            pack_row(
                dims, target.at[g], out_rows.at[g, 0], out_rows.at[g, 1], y, held_row(y).T
            )

    for g in range(groups):
        for item in load_alpha[g]:
            item.wait()
        pack_group(g, lambda y: alpha[y, pl.ds(g * lanes, lanes), :], ring, rows_out)
        if g == 0:
            wait_around(len(partners))
        moves[g][0]()
        if g == 0:
            others[0].wait()
            for y in range(rows):
                kap[depth + y, inner] = jnp.broadcast_to(kappa[y : y + 1, :], (lanes, width)).T
            move_kappa[0]()
    others[1].wait()
    mix[...] = stacked_weights(
        static_blocks(static_vert, levels) * jnp.where(me == 0, static_weight, 0.0)
    )
    for item in load_chi:
        item.wait()
    for y in range(0, rows, 2):
        pair = [chi[y + i] for i in (0, 1)]
        both = mixed(mix, jnp.concatenate(pair, axis=1), 0)
        static[y], static[y + 1] = both[:, :width], both[:, width:]

    for item in others[2:-1]:
        item.wait()
    mix[...] = stacked_weights(vertical_blocks(bounds, lanes, levels, False))
    base[...] = background_ref[...].astype(f32).T

    @pl.loop(0, places // lanes)
    def _(chunk):
        here = pl.ds(pl.multiple_of(chunk * lanes, lanes), lanes)
        anchor = anchor_ref[:, here]
        anchor_row = anchor // band
        anchor_col = anchor - anchor_row * band
        weight = [weight_ref[q : q + 1, here] for q in range(4)]
        slot = lax.broadcasted_iota(jnp.int32, (band, lanes), 0)
        at_left, at_right = slot == anchor_col, slot == anchor_col + 1
        parts = [
            split(
                jnp.where(
                    at_left, weight[2 * d], jnp.where(at_right, weight[2 * d + 1], 0.0)
                )
            )
            for d in range(2)
        ]
        spread_row = jnp.broadcast_to(anchor_row, (shift, lanes))
        for y in range(rows):
            upper = jnp.where(spread_row == y, 1.0, 0.0).astype(bf16)
            lower = jnp.where(spread_row == y - 1, 1.0, 0.0).astype(bf16)
            for half in range(2):
                cut = slice(half * shift, (half + 1) * shift)
                place = pl.ds(half * block + y * shift, shift)
                for ref, term in ((high, 0), (low, 1)):
                    ref[place, here] = parts[0][term][cut] * upper + parts[1][term][cut] * lower
        line = lax.broadcasted_iota(jnp.int32, (rows, lanes), 0)
        past = anchor_col == band - 1
        ends = jnp.where(
            past & (line == anchor_row), weight[1],
            jnp.where(past & (line == anchor_row + 1), weight[3], 0.0),
        )
        final = pl.ds(2 * block, rows)
        high[final, here], low[final, here] = split(ends)

    move_kappa[1]()
    fill_halo_rows(
        dims, kap,
        lambda d: jnp.broadcast_to(kappa_in[0, d : d + 1, :], (lanes, width)).T,
        lambda d: jnp.broadcast_to(
            kappa_in[1, SIDE - depth + d : SIDE - depth + d + 1, :], (lanes, width)
        ).T,
    )

    def diffused(g, source, in_rows, copies):
        copies[g][1]()
        fill_halo_rows(
            dims, source.at[g], lambda d: in_rows[g, 0, d].astype(f32),
            lambda d: in_rows[g, 1, d].astype(f32),
        )
        diffuse(dims, source.at[g], work, kap)
        for y in range(0, rows, 2):
            pair = [source[g, depth + y + i, inner] for i in (0, 1)]
            both = mixed(mix, jnp.concatenate(pair, axis=0), 1)
            for i in (0, 1):
                yield y + i, both[:, i * width : (i + 1) * width]

    for g in range(groups):
        for y, value in diffused(g, ring, rows_in, moves):
            field[pl.ds(g * lanes * pitch + y, lanes, stride=pitch), :] = value
    others[-1].wait()

    def field_rows(k, level):
        return pl.ds(pl.multiple_of((k * levels + level) * pitch, SIDE // 2), rows)

    @pl.loop(0, levels)
    def _(level):
        place = pl.multiple_of(level * rows, rows)
        spreads = [field[field_rows(k, level), :] for k in range(members)]
        for v in range(variables):
            total = perturb[0, v, pl.ds(place, rows), :].astype(f32) * spreads[0]
            for k in range(1, members):
                total = total + perturb[k, v, pl.ds(place, rows), :].astype(f32) * spreads[k]
            nat[field_rows(v, level), :] = total

    for y in range(rows):
        partial[y] = (ens_scale * nat[pl.ds(y, column, stride=pitch), :] + static[y]).T

    def copy(source, target, kind, hop, device):
        return pltpu.make_async_remote_copy(
            src_ref=source, dst_ref=target, send_sem=send.at[kind, hop],
            recv_sem=recv.at[kind, hop], device_id=device, device_id_type=pl.DeviceIdType.MESH,
        )

    def to_partners(source, target, kind, each):
        return [
            copy(source.at[h - 1] if each else source, target.at[h - 1], kind, h, partners[h - 1])
            for h in hops
        ]

    move_rim = copy(rim_out, rim_in, 0, 0, west)
    move_near = to_partners(near_out, near_in, 1, True)
    move_far = to_partners(far_out, far_in, 2, True)
    move_turn = [
        copy(turn_out, turn_in, 1, 0, east), copy(turn_scale, turn_scale_in, 2, 0, east)
    ]
    back_far = to_partners(far_code, far_codes, 3, False)
    back_far += to_partners(far_scale, far_scales, 4, False)
    back_near = to_partners(near_code, near_codes, 5, False)
    back_near += to_partners(near_scale, near_scales, 6, False)

    band_of = band_selector(owner, split_count)
    away = [band_of(lax.rem(me + hop, split_count)) for hop in hops]
    own_band = band_of(me)

    def columns(start):
        return jnp.concatenate([partial[y, pl.ds(start, shift), :] for y in range(rows)], axis=0)

    def edge(start):
        return jnp.concatenate([partial[y, pl.ds(start, 1), :] for y in range(rows)], axis=0)

    def near_of(index):
        return choose(index, [columns(b * band + shift) for b in range(split_count)])

    def far_of(index):
        options = [
            jnp.concatenate([columns(b * band), edge(b * band + shift)], axis=0)
            for b in range(1, split_count)
        ]
        return choose(index, options + [rim_in[...].astype(f32)])

    rim_out[...] = jnp.concatenate([columns(0), edge(shift)], axis=0).astype(bf16)
    move_rim.start()
    for h in hops:
        near_out[h - 1] = near_of(away[h - 1]).astype(bf16)
        move_near[h - 1].start()
    move_rim.wait_recv()
    for h in hops:
        far_out[h - 1] = far_of(away[h - 1]).astype(bf16)
        move_far[h - 1].start()
    near, far = near_of(own_band), far_of(own_band)
    for h in hops:
        move_near[h - 1].wait_recv()
        near = near + near_in[h - 1].astype(f32)
    table[pl.ds(0, block), :] = near.astype(bf16)
    for h in hops:
        move_far[h - 1].wait_recv()
        far = far + far_in[h - 1].astype(f32)
    table[pl.ds(block, block + rows), :] = far.astype(bf16)

    cells = table[...]
    total = base[...] + lax.dot_general(cells, high[...], TN, preferred_element_type=f32)
    total = total + lax.dot_general(cells, low[...], TN, preferred_element_type=f32)
    bent = jnp.tanh(total)
    jacobian = jacobian_ref[...]
    channels = jacobian.shape[0]
    modeled = lax.dot_general(
        stacked_weights(jacobian), jnp.concatenate(split(bent), axis=0), NN,
        preferred_element_type=f32,
    )
    modeled = modeled[:channels] + modeled[channels:]
    position = lax.broadcasted_iota(jnp.int32, modeled.shape, 1)
    misfit = jnp.where(
        position < count[0], (modeled - observed_ref[...]) * inv_var_ref[...], 0.0
    )
    misfit_high = misfit.astype(bf16).astype(f32)
    jacobian_high = jacobian.astype(bf16).astype(f32)
    back = lax.dot_general(
        jnp.concatenate(
            [jacobian_high, jacobian_high, jacobian - jacobian_high, jnp.zeros_like(jacobian)],
            axis=0,
        ).astype(bf16),
        jnp.concatenate(
            [misfit_high, misfit - misfit_high, misfit_high, jnp.zeros_like(misfit)], axis=0
        ).astype(bf16),
        TN, preferred_element_type=f32,
    )
    state_high, state_low = split((1.0 - bent * bent) * back)
    states = jnp.concatenate([state_high, state_low], axis=0)

    def cells_of(start, size):
        here = pl.ds(start, size)
        both = lax.dot_general(high[here, :], states, NT, preferred_element_type=f32)
        rest = lax.dot_general(low[here, :], state_high, NT, preferred_element_type=f32)
        return both[:, :column] + both[:, column:] + rest

    far_code[...], far_scale[...] = coded(cells_of(block, block + rows))
    for item in back_far:
        item.start()
    near_code[...], near_scale[...] = coded(cells_of(0, block))
    for item in back_near:
        item.start()

    def hop_of(index):
        gap = me - owner[0, index]
        return jnp.where(gap < 0, gap + split_count, gap)

    def fars(index, scales):
        own, rest = (far_scale, far_scales) if scales else (far_code, far_codes)
        values = [own[...]] + [rest[h - 1] for h in hops]
        return choose(hop_of(index), values if scales else [v.astype(jnp.int32) for v in values])

    for item in back_far:
        item.wait_recv()
    turn_out[...] = fars(split_count - 1, False).astype(jnp.int16)
    turn_scale[...] = fars(split_count - 1, True)
    for item in move_turn:
        item.start()
    mix[...] = stacked_weights(static_weight * static_blocks(static_vert, levels).T)
    ends = []
    for b in range(split_count - 1):
        value = fars(b, False).astype(f32) * fars(b, True)[:1]
        for y in range(rows):
            grad[y, pl.ds((b + 1) * band, shift), :] = value[y * shift : (y + 1) * shift]
        ends.append(value[block:])
    for item in back_near:
        item.wait_recv()
    nears = [near_code[...]] + [near_codes[h - 1] for h in hops]
    nears = [v.astype(jnp.int32) for v in nears]
    near_steps = [near_scale[...]] + [near_scales[h - 1] for h in hops]
    for b in range(split_count):
        value = choose(hop_of(b), nears).astype(f32) * choose(hop_of(b), near_steps)[:1]
        for y in range(rows):
            grad[y, pl.ds(b * band + shift, shift), :] = value[y * shift : (y + 1) * shift]
    for item in move_turn:
        item.wait_recv()
    turned = turn_in[...].astype(f32) * turn_scale_in[:1]
    for y in range(rows):
        grad[y, pl.ds(0, shift), :] = turned[y * shift : (y + 1) * shift]
    for b, value in enumerate([turned[block:]] + ends):
        place = pl.ds(b * band + shift, 1)
        for y in range(rows):
            grad[y, place, :] = grad[y, place, :] + value[y : y + 1]

    for y in range(rows):
        nat[pl.ds(y, column, stride=pitch), :] = ens_scale * grad[y].T
    for g in range(groups):

        @pl.loop(0, levels)
        def _(level, g=g):
            place = pl.multiple_of(level * rows, rows)
            slopes = [nat[field_rows(v, level), :] for v in range(variables)]
            for k in range(g * group_members, (g + 1) * group_members):
                total = perturb[k, 0, pl.ds(place, rows), :].astype(f32) * slopes[0]
                for v in range(1, variables):
                    total = total + perturb[k, v, pl.ds(place, rows), :].astype(f32) * slopes[v]
                field[field_rows(k, level), :] = total * kappa[...]

        pack_group(
            g, lambda y: field[pl.ds(g * lanes * pitch + y, lanes, stride=pitch), :], back_ring,
            back_rows_out,
        )
        back_moves[g][0]()
    for y in range(0, rows, 2):
        both = mixed(mix, jnp.concatenate([grad[y], grad[y + 1]], axis=0), 1)
        for i in (0, 1):
            out_chi[y + i] = chi[y + i] + both[:, i * width : (i + 1) * width]
    mix[...] = stacked_weights(vertical_blocks(bounds, lanes, levels, True))
    inverse = 1.0 / kappa[...]
    for g in range(groups):
        here = pl.ds(g * lanes, lanes)
        for y, value in diffused(g, back_ring, back_rows_in, back_moves):
            out_alpha[y, here, :] = alpha[y, here, :] + inverse[y : y + 1] * value
    for item in [move_rim] + move_turn + move_near + move_far + back_near + back_far:
        item.wait_send()


def body(
    alpha, perturb, chi, kappa, vert_bounds, static_vert, fine_owner, obs_stencil, obs_weight,
    background, observed, inv_var, jacobian, obs_count,
):
    members, levels, rows, width = alpha.shape
    variables = perturb.shape[1]
    column = variables * levels
    depth = NDIFF
    count = rows * levels
    dims = (rows, levels, width, variables, depth)
    ens_scale = ensemble_weight / math.sqrt(members * lax.axis_size("mem") - 1)
    split_count = lax.axis_size("mem")
    places = obs_stencil.shape[0]
    shift = width // split_count // 2
    block = rows * shift
    grouped = members * levels // column
    ring_shape = (rows + 2 * depth, width + 4 * SIDE, column)
    smem = pl.BlockSpec(memory_space=pltpu.SMEM)
    vmem = pl.BlockSpec(memory_space=pltpu.VMEM)
    hbm = pl.BlockSpec(memory_space=pltpu.HBM)
    rings = pltpu.VMEM((grouped,) + ring_shape, f32)
    row_pairs = pltpu.VMEM((grouped, 2, depth, width, column), bf16)
    pitch = rows + SIDE // 2
    alpha_shape, chi_shape = (rows, members * levels, width), (rows, column, width)
    near, far = (block, column), (block + rows, column)
    scale = (SIDE, column)
    away = (split_count - 1,)
    i16 = jnp.int16
    grad_alpha, grad_chi = pl.pallas_call(
        lambda *refs: step_kernel(dims, ens_scale, *refs),
        in_specs=[smem, smem] + [hbm] * 12,
        out_specs=[vmem, vmem],
        out_shape=[
            jax.ShapeDtypeStruct(alpha_shape, f32), jax.ShapeDtypeStruct(chi_shape, f32)
        ],
        scratch_shapes=[
            pltpu.VMEM(alpha_shape, f32),
            pltpu.VMEM(chi_shape, f32),
            pltpu.VMEM((members, variables, count, width), bf16),
            pltpu.VMEM(kappa.shape, f32),
            pltpu.VMEM(static_vert.shape, f32),
            pltpu.VMEM(vert_bounds.shape, jnp.int32),
            pltpu.VMEM(jacobian.shape, f32),
            pltpu.VMEM((1, places), jnp.int32),
            pltpu.VMEM((4, places), f32),
            pltpu.VMEM((places, column), bf16),
            pltpu.VMEM(observed.shape, f32),
            pltpu.VMEM(inv_var.shape, f32),
            pltpu.VMEM(ring_shape, f32),
            rings,
            rings,
            pltpu.VMEM(ring_shape, f32),
            row_pairs,
            row_pairs,
            row_pairs,
            row_pairs,
            pltpu.VMEM((2, SIDE, width), f32),
            pltpu.VMEM((members * levels * pitch, width), f32),
            pltpu.VMEM((column * pitch, width), f32),
            pltpu.VMEM((rows, column, width), f32),
            pltpu.VMEM((2 * column, 2 * column), bf16),
            pltpu.VMEM((rows, width, column), f32),
            pltpu.VMEM((2 * block + rows, places), bf16),
            pltpu.VMEM((2 * block + rows, places), bf16),
            pltpu.VMEM((2 * block + rows, column), bf16),
            pltpu.VMEM((column, places), f32),
            pltpu.VMEM(far, bf16),
            pltpu.VMEM(far, bf16),
            pltpu.VMEM(away + near, bf16),
            pltpu.VMEM(away + near, bf16),
            pltpu.VMEM(away + far, bf16),
            pltpu.VMEM(away + far, bf16),
            pltpu.VMEM(near, i16),
            pltpu.VMEM(scale, f32),
            pltpu.VMEM(far, i16),
            pltpu.VMEM(scale, f32),
            pltpu.VMEM(away + near, i16),
            pltpu.VMEM(away + scale, f32),
            pltpu.VMEM(away + far, i16),
            pltpu.VMEM(away + scale, f32),
            pltpu.VMEM(far, i16),
            pltpu.VMEM(scale, f32),
            pltpu.VMEM(far, i16),
            pltpu.VMEM(scale, f32),
            pltpu.VMEM((rows, width, column), f32),
            pltpu.SemaphoreType.DMA(((grouped + 1) * rows + 10,)),
            pltpu.SemaphoreType.DMA((7, split_count)),
            pltpu.SemaphoreType.DMA((7, split_count)),
            pltpu.SemaphoreType.DMA((2 * grouped + 1, 8)),
            pltpu.SemaphoreType.DMA((2 * grouped + 1, 8)),
        ],
        compiler_params=pltpu.CompilerParams(
            collective_id=0, has_side_effects=True, vmem_limit_bytes=44 << 20
        ),
        name="step",
    )(
        fine_owner, obs_count,
        *[
            pltpu.with_memory_space_constraint(value, pltpu.HBM)
            for value in (
                alpha.reshape(members * levels, rows, width), chi.reshape(column, rows, width),
                perturb.reshape(members, variables, count, width), kappa, static_vert, vert_bounds,
                jacobian, obs_stencil.reshape(1, places), obs_weight, background, observed, inv_var,
            )
        ],
    )
    alpha_out, chi_out = (members * levels, rows, width), (column, rows, width)
    grad_alpha, grad_chi = pl.pallas_call(
        unpack_kernel,
        in_specs=[vmem, vmem],
        out_specs=[hbm, hbm],
        out_shape=[jax.ShapeDtypeStruct(alpha_out, f32), jax.ShapeDtypeStruct(chi_out, f32)],
        scratch_shapes=[pltpu.SemaphoreType.DMA((2, rows))],
        compiler_params=pltpu.CompilerParams(vmem_limit_bytes=16 << 20),
        name="unpack",
    )(grad_alpha, grad_chi)
    return grad_alpha.reshape(alpha.shape), grad_chi.reshape(chi.shape)


def solution(mesh):
    in_specs = (
        P("mem", None, "gy", "gx"),
        P("mem", None, None, "gy", "gx"),
        P(None, None, "gy", "gx"),
        P("gy", "gx"),
        P(),
        P(),
        P(("gy", "gx"), None),
        P(("mem", "gy", "gx")),
        P(None, ("mem", "gy", "gx")),
        P(("mem", "gy", "gx"), None),
        P(None, ("mem", "gy", "gx")),
        P(None, ("mem", "gy", "gx")),
        P(),
        P(("mem", "gy", "gx")),
    )
    out_specs = (P("mem", None, "gy", "gx"), P(None, None, "gy", "gx"))
    return jax.shard_map(body, mesh=mesh, in_specs=in_specs, out_specs=out_specs, check_vma=False)
```

```python
import math

import jax
import jax.numpy as jnp
from jax import lax
from jax.experimental import pallas as pl
from jax.experimental.pallas import tpu as pltpu
from jax.sharding import PartitionSpec as P

NDIFF = 4

ensemble_weight = 0.8
static_weight = 0.6
vertical_scale = 2.0
code_limit = 32767.0
f32 = jnp.float32
bf16 = jnp.bfloat16
SIDE = 8
NN = (((1,), (0,)), ((), ()))
NT = (((1,), (1,)), ((), ()))
TN = (((0,), (0,)), ((), ()))


def compass():
    gx, gy = lax.axis_index("gx"), lax.axis_index("gy")
    gx_count, gy_count = lax.axis_size("gx"), lax.axis_size("gy")
    east, west = lax.rem(gx + 1, gx_count), lax.rem(gx + gx_count - 1, gx_count)
    return east, west, gy - 1, gy + 1, gy > 0, gy < gy_count - 1


def greet_around(partners):
    east, west, north, south, has_north, has_south = compass()
    barrier = pltpu.get_barrier_semaphore()

    def greet(device):
        pl.semaphore_signal(
            barrier, inc=1, device_id=device, device_id_type=pl.DeviceIdType.MESH
        )

    for device in [{"gx": east}, {"gx": west}] + partners:
        greet(device)

    @pl.when(has_north)
    def _():
        for device in ({"gy": north}, {"gy": north, "gx": east}, {"gy": north, "gx": west}):
            greet(device)

    @pl.when(has_south)
    def _():
        for device in ({"gy": south}, {"gy": south, "gx": east}, {"gy": south, "gx": west}):
            greet(device)


def wait_around(partners):
    east, west, north, south, has_north, has_south = compass()
    peers = partners + 2 + 3 * has_north.astype(jnp.int32) + 3 * has_south.astype(jnp.int32)
    pl.semaphore_wait(pltpu.get_barrier_semaphore(), peers)


def ring_copies(dims, ring, corners, first_rows, last_rows, south_in, north_in, send, recv):
    rows, levels, width, variables, depth = dims
    east, west, north, south, has_north, has_south = compass()
    body, above, below = pl.ds(depth, rows), pl.ds(0, depth), pl.ds(depth + rows, depth)
    first, last = pl.ds(2 * SIDE, depth), pl.ds(2 * SIDE + width - depth, depth)
    before, after = pl.ds(2 * SIDE - depth, depth), pl.ds(2 * SIDE + width, depth)
    left, right = pl.ds(0, depth), pl.ds(SIDE - depth, depth)

    def copy(source, target, place, device):
        return pltpu.make_async_remote_copy(
            src_ref=source, dst_ref=target, send_sem=send.at[place], recv_sem=recv.at[place],
            device_id=device, device_id_type=pl.DeviceIdType.MESH,
        )

    across = [
        copy(ring.at[body, last], ring.at[body, before], 0, {"gx": east}),
        copy(ring.at[body, first], ring.at[body, after], 1, {"gx": west}),
    ]
    up = [
        copy(first_rows, south_in, 2, {"gy": north}),
        copy(corners.at[0, :, right], ring.at[below, before], 3, {"gy": north, "gx": east}),
        copy(corners.at[1, :, left], ring.at[below, after], 4, {"gy": north, "gx": west}),
    ]
    down = [
        copy(last_rows, north_in, 5, {"gy": south}),
        copy(corners.at[2, :, right], ring.at[above, before], 6, {"gy": south, "gx": east}),
        copy(corners.at[3, :, left], ring.at[above, after], 7, {"gy": south, "gx": west}),
    ]

    def start():
        for item in across:
            item.start()

        @pl.when(has_north)
        def _():
            for item in up:
                item.start()

        @pl.when(has_south)
        def _():
            for item in down:
                item.start()

    def wait_across():
        for item in across:
            item.wait_recv()
            item.wait_send()

    def wait_rows():
        @pl.when(has_north)
        def _():
            for item in down:
                item.wait_recv()
            for item in up:
                item.wait_send()

        @pl.when(has_south)
        def _():
            for item in up:
                item.wait_recv()
            for item in down:
                item.wait_send()

    return start, wait_across, wait_rows


def save_corners(dims, ring, corners):
    rows, levels, width, variables, depth = dims
    for i, y in enumerate((depth, depth, rows, rows)):
        x = 2 * SIDE if i % 2 else SIDE + width
        corners[i] = ring[pl.ds(y, depth), pl.ds(x, SIDE)]


def mirror_rows(dims, ring):
    rows, levels, width, variables, depth = dims
    east, west, north, south, has_north, has_south = compass()
    whole = pl.ds(SIDE, width + 2 * SIDE)

    @pl.when(jnp.logical_not(has_south))
    def _():
        for d in range(depth):
            ring[depth + rows + d, whole] = ring[depth + rows - 1 - d, whole]

    @pl.when(jnp.logical_not(has_north))
    def _():
        for d in range(depth):
            ring[d, whole] = ring[2 * depth - 1 - d, whole]


def fill_halo_rows(dims, ring, from_south, from_north):
    rows, levels, width, variables, depth = dims
    east, west, north, south, has_north, has_south = compass()
    inner = pl.ds(2 * SIDE, width)

    @pl.when(has_south)
    def _():
        for d in range(depth):
            ring[depth + rows + d, inner] = from_south(d)

    @pl.when(has_north)
    def _():
        for d in range(depth):
            ring[d, inner] = from_north(d)


def diffuse(dims, ring, work, kap, inside):
    rows, levels, width, variables, depth = dims
    for step in range(1, depth + 1):
        source, target = (ring, work) if step % 2 else (work, ring)
        start, stop = (SIDE, width + 3 * SIDE) if step < depth else (2 * SIDE, width + 2 * SIDE)
        if inside:
            count, first, skip = rows // 2 - step, depth + step, 0
        else:
            count, first, skip = depth, step, rows - 2 * step

        @pl.loop(0, count)
        def _(
            pair, source=source, target=target, start=start, stop=stop, first=first, skip=skip,
            count=count,
        ):
            y = first + 2 * pair
            if skip:
                y = y + jnp.where(pair >= count // 2, skip, 0)
            for x in range(start, stop, 6 * SIDE):
                size = min(6 * SIDE, stop - x)
                here = pl.ds(x, size)
                held = [source[y + i, here] for i in (-1, 0, 1, 2)]
                for i in (0, 1):
                    center = held[i + 1]
                    sides = source[y + i, pl.ds(x - 1, size)] + source[y + i, pl.ds(x + 1, size)]
                    change = (held[i] + held[i + 2]) + sides - 4.0 * center
                    target[y + i, here] = center + kap[y + i, here] * change


def split(value):
    high = value.astype(bf16)
    return high, (value - high.astype(f32)).astype(bf16)


def stacked_weights(weights):
    high, low = split(weights)
    return jnp.concatenate(
        [
            jnp.concatenate([high, high], axis=1),
            jnp.concatenate([low, jnp.zeros_like(low)], axis=1),
        ],
        axis=0,
    )


def mixed(weights_ref, value, axis):
    half = weights_ref.shape[0] // 2
    numbers = NT if axis else NN
    both = lax.dot_general(
        weights_ref[...], jnp.concatenate(split(value), axis=axis), numbers,
        preferred_element_type=f32,
    )
    return both[:half] + both[half:]


def lane_grid(lanes, levels):
    row = lax.broadcasted_iota(jnp.int32, (lanes, lanes), 0)
    col = lax.broadcasted_iota(jnp.int32, (lanes, lanes), 1)
    row_block, col_block = row // levels, col // levels
    return row - row_block * levels, col - col_block * levels, row_block == col_block


def vertical_blocks(bounds_ref, lanes, levels, transposed):
    row, col, same = lane_grid(lanes, levels)
    bounds = bounds_ref[...].astype(f32)
    limits = []
    for side in range(2):
        line = jnp.concatenate([bounds[side : side + 1]] * (lanes // levels), axis=1)
        spread = jnp.broadcast_to(line, (lanes, lanes))
        limits.append(spread if transposed else spread.T)
    reach = (row if transposed else col).astype(f32)
    distance = jnp.abs(row - col).astype(f32)
    inside = same & (reach >= limits[0]) & (reach <= limits[1])
    return jnp.where(inside, jnp.exp(-distance / vertical_scale), 0.0)


def static_blocks(static_ref, levels):
    variables = static_ref.shape[0]
    lanes = variables * levels
    same = lane_grid(lanes, levels)[2]
    tiles = [jnp.concatenate([static_ref[v]] * variables, axis=1) for v in range(variables)]
    return jnp.where(same, jnp.concatenate(tiles, axis=0), 0.0)


def pack_row(dims, ring, first_rows, last_rows, y, value):
    rows, levels, width, variables, depth = dims
    ring[depth + y, pl.ds(2 * SIDE, width)] = value
    if y < depth:
        first_rows[y] = value.astype(bf16)
    if y >= rows - depth:
        last_rows[y - (rows - depth)] = value.astype(bf16)


def band_selector(owner, groups):
    def band_of(group):
        result = 0
        for b in range(groups):
            result = result + jnp.where(owner[0, b] == group, b, 0)
        return result

    return band_of


def choose(index, options):
    result = options[0]
    for place in range(1, len(options)):
        result = jnp.where(index == place, options[place], result)
    return result


def coded(value):
    largest = jnp.maximum(jnp.max(jnp.abs(value), axis=0, keepdims=True), 1e-30)
    codes = jnp.round(value * (code_limit / largest)).astype(jnp.int16)
    return codes, jnp.broadcast_to(largest * (1.0 / code_limit), (SIDE, value.shape[1]))


def unpack_kernel(alpha_rows, chi_rows, out_alpha, out_chi, done):
    rows = alpha_rows.shape[0]
    moves = []
    for i, (source, target) in enumerate([(alpha_rows, out_alpha), (chi_rows, out_chi)]):
        moves += [
            pltpu.make_async_copy(source.at[y], target.at[:, y, :], done.at[i, y])
            for y in range(rows)
        ]
    for item in moves:
        item.start()
    for item in moves:
        item.wait()


def step_kernel(
    dims, ens_scale, owner, count, alpha_hbm, chi_hbm, perturb_hbm, kappa_hbm, static_hbm,
    bounds_hbm, jacobian_hbm, anchor_hbm, weight_hbm, background_hbm, observed_hbm, inv_var_hbm,
    out_alpha, out_chi, alpha, chi, perturb, kappa, static_vert, bounds, jacobian_ref, anchor_ref,
    weight_ref, background_ref, observed_ref, inv_var_ref, kap,
    ring, back_ring, work, corners, rows_out, rows_in, back_rows_out, back_rows_in, kappa_in, field, nat,
    static, mix, partial, high, low, table, base, rim_out, rim_in, near_out, near_in, far_out,
    far_in, near_code, near_scale, far_code, far_scale, near_codes, near_scales, far_codes,
    far_scales, turn_out, turn_scale, turn_in, turn_scale_in, grad, load, send, recv, ring_send,
    ring_recv,
):
    rows, levels, width, variables, depth = dims
    groups, lanes = ring.shape[0], ring.shape[3]
    column = variables * levels
    group_members = lanes // levels
    pitch = rows + SIDE // 2
    members = perturb.shape[0]
    inner = pl.ds(2 * SIDE, width)
    split_count = lax.axis_size("mem")
    me, gx, gx_count = lax.axis_index("mem"), lax.axis_index("gx"), lax.axis_size("gx")
    east, west = {"gx": lax.rem(gx + 1, gx_count)}, {"gx": lax.rem(gx + gx_count - 1, gx_count)}
    hops = range(1, split_count)
    partners = [{"mem": lax.rem(me + hop, split_count)} for hop in hops]
    band = width // split_count
    shift = band // 2
    block = rows * shift
    places = anchor_ref.shape[1]

    greet_around(partners)
    load_alpha = [
        [
            pltpu.make_async_copy(
                alpha_hbm.at[pl.ds(g * lanes, lanes), y, :],
                alpha.at[y, pl.ds(g * lanes, lanes), :], load.at[g * rows + y],
            )
            for y in range(rows)
        ]
        for g in range(groups)
    ]
    used = groups * rows
    load_chi = [
        pltpu.make_async_copy(chi_hbm.at[:, y, :], chi.at[y], load.at[used + y])
        for y in range(rows)
    ]
    used += rows
    pairs = [
        (kappa_hbm, kappa), (static_hbm, static_vert), (bounds_hbm, bounds),
        (jacobian_hbm, jacobian_ref), (anchor_hbm, anchor_ref), (weight_hbm, weight_ref),
        (background_hbm, background_ref), (observed_hbm, observed_ref), (inv_var_hbm, inv_var_ref),
        (perturb_hbm, perturb),
    ]
    others = [
        pltpu.make_async_copy(source, target, load.at[used + i])
        for i, (source, target) in enumerate(pairs)
    ]
    for item in load_alpha[0] + others[:1]:
        item.start()
    for part in load_alpha[1:] + [load_chi, others[1:]]:
        for item in part:
            item.start()

    def ring_moves(target, out_rows, in_rows, first):
        return [
            ring_copies(
                dims, target.at[g], corners.at[first + g], out_rows.at[g, 0], out_rows.at[g, 1],
                in_rows.at[g, 0], in_rows.at[g, 1], ring_send.at[first + g], ring_recv.at[first + g],
            )
            for g in range(groups)
        ]

    moves = ring_moves(ring, rows_out, rows_in, 0)
    back_moves = ring_moves(back_ring, back_rows_out, back_rows_in, groups)
    move_kappa = ring_copies(
        dims, kap, corners.at[2 * groups], kappa.at[pl.ds(0, SIDE)],
        kappa.at[pl.ds(rows - SIDE, SIDE)], kappa_in.at[0], kappa_in.at[1], ring_send.at[2 * groups], ring_recv.at[2 * groups],
    )

    def pack_group(g, held_row, target, out_rows, place):
        for y in range(rows):
            pack_row(
                dims, target.at[g], out_rows.at[g, 0], out_rows.at[g, 1], y, held_row(y).T
            )
        save_corners(dims, target.at[g], corners.at[place + g])

    for g in range(groups):
        for item in load_alpha[g]:
            item.wait()
        pack_group(g, lambda y: alpha[y, pl.ds(g * lanes, lanes), :], ring, rows_out, 0)
        if g == 0:
            wait_around(len(partners))
        moves[g][0]()
        if g == 0:
            others[0].wait()
            for y in range(rows):
                kap[depth + y, inner] = jnp.broadcast_to(kappa[y : y + 1, :], (lanes, width)).T
            save_corners(dims, kap, corners.at[2 * groups])
            move_kappa[0]()
    others[1].wait()
    mix[...] = stacked_weights(
        static_blocks(static_vert, levels) * jnp.where(me == 0, static_weight, 0.0)
    )
    for item in load_chi:
        item.wait()
    for y in range(0, rows, 2):
        pair = [chi[y + i] for i in (0, 1)]
        both = mixed(mix, jnp.concatenate(pair, axis=1), 0)
        static[y], static[y + 1] = both[:, :width], both[:, width:]

    for item in others[2:-1]:
        item.wait()
    mix[...] = stacked_weights(vertical_blocks(bounds, lanes, levels, False))
    base[...] = background_ref[...].astype(f32).T

    @pl.loop(0, places // lanes)
    def _(chunk):
        here = pl.ds(pl.multiple_of(chunk * lanes, lanes), lanes)
        anchor = anchor_ref[:, here]
        anchor_row = anchor // band
        anchor_col = anchor - anchor_row * band
        weight = [weight_ref[q : q + 1, here] for q in range(4)]
        slot = lax.broadcasted_iota(jnp.int32, (band, lanes), 0)
        at_left, at_right = slot == anchor_col, slot == anchor_col + 1
        parts = [
            split(
                jnp.where(
                    at_left, weight[2 * d], jnp.where(at_right, weight[2 * d + 1], 0.0)
                )
            )
            for d in range(2)
        ]
        spread_row = jnp.broadcast_to(anchor_row, (shift, lanes))
        for y in range(rows):
            upper = jnp.where(spread_row == y, 1.0, 0.0).astype(bf16)
            lower = jnp.where(spread_row == y - 1, 1.0, 0.0).astype(bf16)
            for half in range(2):
                cut = slice(half * shift, (half + 1) * shift)
                place = pl.ds(half * block + y * shift, shift)
                for ref, term in ((high, 0), (low, 1)):
                    ref[place, here] = parts[0][term][cut] * upper + parts[1][term][cut] * lower
        line = lax.broadcasted_iota(jnp.int32, (rows, lanes), 0)
        past = anchor_col == band - 1
        ends = jnp.where(
            past & (line == anchor_row), weight[1],
            jnp.where(past & (line == anchor_row + 1), weight[3], 0.0),
        )
        final = pl.ds(2 * block, rows)
        high[final, here], low[final, here] = split(ends)

    move_kappa[1]()
    mirror_rows(dims, kap)

    def diffuse_inside(source, copies):
        for g in range(groups):
            copies[g][1]()
            mirror_rows(dims, source.at[g])
            diffuse(dims, source.at[g], work.at[g], kap, True)

    diffuse_inside(ring, moves)
    move_kappa[2]()
    fill_halo_rows(
        dims, kap,
        lambda d: jnp.broadcast_to(kappa_in[0, d : d + 1, :], (lanes, width)).T,
        lambda d: jnp.broadcast_to(
            kappa_in[1, SIDE - depth + d : SIDE - depth + d + 1, :], (lanes, width)
        ).T,
    )

    def diffused(g, source, in_rows, copies):
        copies[g][2]()
        fill_halo_rows(
            dims, source.at[g], lambda d: in_rows[g, 0, d].astype(f32),
            lambda d: in_rows[g, 1, d].astype(f32),
        )
        diffuse(dims, source.at[g], work.at[g], kap, False)
        for y in range(0, rows, 2):
            pair = [source[g, depth + y + i, inner] for i in (0, 1)]
            both = mixed(mix, jnp.concatenate(pair, axis=0), 1)
            for i in (0, 1):
                yield y + i, both[:, i * width : (i + 1) * width]

    for g in range(groups):
        for y, value in diffused(g, ring, rows_in, moves):
            field[pl.ds(g * lanes * pitch + y, lanes, stride=pitch), :] = value
    others[-1].wait()

    def field_rows(k, level):
        return pl.ds(pl.multiple_of((k * levels + level) * pitch, SIDE // 2), rows)

    @pl.loop(0, levels)
    def _(level):
        place = pl.multiple_of(level * rows, rows)
        spreads = [field[field_rows(k, level), :] for k in range(members)]
        for v in range(variables):
            total = perturb[0, v, pl.ds(place, rows), :].astype(f32) * spreads[0]
            for k in range(1, members):
                total = total + perturb[k, v, pl.ds(place, rows), :].astype(f32) * spreads[k]
            nat[field_rows(v, level), :] = total

    for y in range(rows):
        partial[y] = (ens_scale * nat[pl.ds(y, column, stride=pitch), :] + static[y]).T

    def copy(source, target, kind, hop, device):
        return pltpu.make_async_remote_copy(
            src_ref=source, dst_ref=target, send_sem=send.at[kind, hop],
            recv_sem=recv.at[kind, hop], device_id=device, device_id_type=pl.DeviceIdType.MESH,
        )

    def to_partners(source, target, kind, each):
        return [
            copy(source.at[h - 1] if each else source, target.at[h - 1], kind, h, partners[h - 1])
            for h in hops
        ]

    move_rim = copy(rim_out, rim_in, 0, 0, west)
    move_near = to_partners(near_out, near_in, 1, True)
    move_far = to_partners(far_out, far_in, 2, True)
    move_turn = [
        copy(turn_out, turn_in, 1, 0, east), copy(turn_scale, turn_scale_in, 2, 0, east)
    ]
    back_far = to_partners(far_code, far_codes, 3, False)
    back_far += to_partners(far_scale, far_scales, 4, False)
    back_near = to_partners(near_code, near_codes, 5, False)
    back_near += to_partners(near_scale, near_scales, 6, False)

    band_of = band_selector(owner, split_count)
    away = [band_of(lax.rem(me + hop, split_count)) for hop in hops]
    own_band = band_of(me)

    def columns(start):
        return jnp.concatenate([partial[y, pl.ds(start, shift), :] for y in range(rows)], axis=0)

    def edge(start):
        return jnp.concatenate([partial[y, pl.ds(start, 1), :] for y in range(rows)], axis=0)

    def near_of(index):
        return choose(index, [columns(b * band + shift) for b in range(split_count)])

    def far_of(index):
        options = [
            jnp.concatenate([columns(b * band), edge(b * band + shift)], axis=0)
            for b in range(1, split_count)
        ]
        return choose(index, options + [rim_in[...].astype(f32)])

    rim_out[...] = jnp.concatenate([columns(0), edge(shift)], axis=0).astype(bf16)
    move_rim.start()
    for h in hops:
        near_out[h - 1] = near_of(away[h - 1]).astype(bf16)
        move_near[h - 1].start()
    move_rim.wait_recv()
    for h in hops:
        far_out[h - 1] = far_of(away[h - 1]).astype(bf16)
        move_far[h - 1].start()
    near, far = near_of(own_band), far_of(own_band)
    for h in hops:
        move_near[h - 1].wait_recv()
        near = near + near_in[h - 1].astype(f32)
    table[pl.ds(0, block), :] = near.astype(bf16)
    for h in hops:
        move_far[h - 1].wait_recv()
        far = far + far_in[h - 1].astype(f32)
    table[pl.ds(block, block + rows), :] = far.astype(bf16)

    cells = table[...]
    total = base[...] + lax.dot_general(cells, high[...], TN, preferred_element_type=f32)
    total = total + lax.dot_general(cells, low[...], TN, preferred_element_type=f32)
    bent = jnp.tanh(total)
    jacobian = jacobian_ref[...]
    channels = jacobian.shape[0]
    modeled = lax.dot_general(
        stacked_weights(jacobian), jnp.concatenate(split(bent), axis=0), NN,
        preferred_element_type=f32,
    )
    modeled = modeled[:channels] + modeled[channels:]
    position = lax.broadcasted_iota(jnp.int32, modeled.shape, 1)
    misfit = jnp.where(
        position < count[0], (modeled - observed_ref[...]) * inv_var_ref[...], 0.0
    )
    misfit_high = misfit.astype(bf16).astype(f32)
    jacobian_high = jacobian.astype(bf16).astype(f32)
    back = lax.dot_general(
        jnp.concatenate(
            [jacobian_high, jacobian_high, jacobian - jacobian_high, jnp.zeros_like(jacobian)],
            axis=0,
        ).astype(bf16),
        jnp.concatenate(
            [misfit_high, misfit - misfit_high, misfit_high, jnp.zeros_like(misfit)], axis=0
        ).astype(bf16),
        TN, preferred_element_type=f32,
    )
    state_high, state_low = split((1.0 - bent * bent) * back)
    states = jnp.concatenate([state_high, state_low], axis=0)

    def cells_of(start, size):
        here = pl.ds(start, size)
        both = lax.dot_general(high[here, :], states, NT, preferred_element_type=f32)
        rest = lax.dot_general(low[here, :], state_high, NT, preferred_element_type=f32)
        return both[:, :column] + both[:, column:] + rest

    far_code[...], far_scale[...] = coded(cells_of(block, block + rows))
    for item in back_far:
        item.start()
    near_code[...], near_scale[...] = coded(cells_of(0, block))
    for item in back_near:
        item.start()

    def hop_of(index):
        gap = me - owner[0, index]
        return jnp.where(gap < 0, gap + split_count, gap)

    def fars(index, scales):
        own, rest = (far_scale, far_scales) if scales else (far_code, far_codes)
        values = [own[...]] + [rest[h - 1] for h in hops]
        return choose(hop_of(index), values if scales else [v.astype(jnp.int32) for v in values])

    for item in back_far:
        item.wait_recv()
    turn_out[...] = fars(split_count - 1, False).astype(jnp.int16)
    turn_scale[...] = fars(split_count - 1, True)
    for item in move_turn:
        item.start()
    mix[...] = stacked_weights(static_weight * static_blocks(static_vert, levels).T)
    ends = []
    for b in range(split_count - 1):
        value = fars(b, False).astype(f32) * fars(b, True)[:1]
        for y in range(rows):
            grad[y, pl.ds((b + 1) * band, shift), :] = value[y * shift : (y + 1) * shift]
        ends.append(value[block:])
    for item in back_near:
        item.wait_recv()
    nears = [near_code[...]] + [near_codes[h - 1] for h in hops]
    nears = [v.astype(jnp.int32) for v in nears]
    near_steps = [near_scale[...]] + [near_scales[h - 1] for h in hops]
    for b in range(split_count):
        value = choose(hop_of(b), nears).astype(f32) * choose(hop_of(b), near_steps)[:1]
        for y in range(rows):
            grad[y, pl.ds(b * band + shift, shift), :] = value[y * shift : (y + 1) * shift]
    for item in move_turn:
        item.wait_recv()
    turned = turn_in[...].astype(f32) * turn_scale_in[:1]
    for y in range(rows):
        grad[y, pl.ds(0, shift), :] = turned[y * shift : (y + 1) * shift]
    for b, value in enumerate([turned[block:]] + ends):
        place = pl.ds(b * band + shift, 1)
        for y in range(rows):
            grad[y, place, :] = grad[y, place, :] + value[y : y + 1]

    for y in range(rows):
        nat[pl.ds(y, column, stride=pitch), :] = ens_scale * grad[y].T
    for g in range(groups):

        @pl.loop(0, levels)
        def _(level, g=g):
            place = pl.multiple_of(level * rows, rows)
            slopes = [nat[field_rows(v, level), :] for v in range(variables)]
            for k in range(g * group_members, (g + 1) * group_members):
                total = perturb[k, 0, pl.ds(place, rows), :].astype(f32) * slopes[0]
                for v in range(1, variables):
                    total = total + perturb[k, v, pl.ds(place, rows), :].astype(f32) * slopes[v]
                field[field_rows(k, level), :] = total * kappa[...]

        pack_group(
            g, lambda y: field[pl.ds(g * lanes * pitch + y, lanes, stride=pitch), :], back_ring,
            back_rows_out, groups,
        )
        back_moves[g][0]()
    for y in range(0, rows, 2):
        both = mixed(mix, jnp.concatenate([grad[y], grad[y + 1]], axis=0), 1)
        for i in (0, 1):
            out_chi[y + i] = chi[y + i] + both[:, i * width : (i + 1) * width]
    mix[...] = stacked_weights(vertical_blocks(bounds, lanes, levels, True))
    inverse = 1.0 / kappa[...]
    diffuse_inside(back_ring, back_moves)
    for g in range(groups):
        here = pl.ds(g * lanes, lanes)
        for y, value in diffused(g, back_ring, back_rows_in, back_moves):
            out_alpha[y, here, :] = alpha[y, here, :] + inverse[y : y + 1] * value
    for item in [move_rim] + move_turn + move_near + move_far + back_near + back_far:
        item.wait_send()


def body(
    alpha, perturb, chi, kappa, vert_bounds, static_vert, fine_owner, obs_stencil, obs_weight,
    background, observed, inv_var, jacobian, obs_count,
):
    members, levels, rows, width = alpha.shape
    variables = perturb.shape[1]
    column = variables * levels
    depth = NDIFF
    count = rows * levels
    dims = (rows, levels, width, variables, depth)
    ens_scale = ensemble_weight / math.sqrt(members * lax.axis_size("mem") - 1)
    split_count = lax.axis_size("mem")
    places = obs_stencil.shape[0]
    shift = width // split_count // 2
    block = rows * shift
    grouped = members * levels // column
    ring_shape = (rows + 2 * depth, width + 4 * SIDE, column)
    smem = pl.BlockSpec(memory_space=pltpu.SMEM)
    vmem = pl.BlockSpec(memory_space=pltpu.VMEM)
    hbm = pl.BlockSpec(memory_space=pltpu.HBM)
    rings = pltpu.VMEM((grouped,) + ring_shape, f32)
    row_pairs = pltpu.VMEM((grouped, 2, depth, width, column), bf16)
    pitch = rows + SIDE // 2
    alpha_shape, chi_shape = (rows, members * levels, width), (rows, column, width)
    near, far = (block, column), (block + rows, column)
    scale = (SIDE, column)
    away = (split_count - 1,)
    i16 = jnp.int16
    grad_alpha, grad_chi = pl.pallas_call(
        lambda *refs: step_kernel(dims, ens_scale, *refs),
        in_specs=[smem, smem] + [hbm] * 12,
        out_specs=[vmem, vmem],
        out_shape=[
            jax.ShapeDtypeStruct(alpha_shape, f32), jax.ShapeDtypeStruct(chi_shape, f32)
        ],
        scratch_shapes=[
            pltpu.VMEM(alpha_shape, f32),
            pltpu.VMEM(chi_shape, f32),
            pltpu.VMEM((members, variables, count, width), bf16),
            pltpu.VMEM(kappa.shape, f32),
            pltpu.VMEM(static_vert.shape, f32),
            pltpu.VMEM(vert_bounds.shape, jnp.int32),
            pltpu.VMEM(jacobian.shape, f32),
            pltpu.VMEM((1, places), jnp.int32),
            pltpu.VMEM((4, places), f32),
            pltpu.VMEM((places, column), bf16),
            pltpu.VMEM(observed.shape, f32),
            pltpu.VMEM(inv_var.shape, f32),
            pltpu.VMEM(ring_shape, f32),
            rings,
            rings,
            rings,
            pltpu.VMEM((2 * grouped + 1, 4, depth, SIDE, column), f32),
            row_pairs,
            row_pairs,
            row_pairs,
            row_pairs,
            pltpu.VMEM((2, SIDE, width), f32),
            pltpu.VMEM((members * levels * pitch, width), f32),
            pltpu.VMEM((column * pitch, width), f32),
            pltpu.VMEM((rows, column, width), f32),
            pltpu.VMEM((2 * column, 2 * column), bf16),
            pltpu.VMEM((rows, width, column), f32),
            pltpu.VMEM((2 * block + rows, places), bf16),
            pltpu.VMEM((2 * block + rows, places), bf16),
            pltpu.VMEM((2 * block + rows, column), bf16),
            pltpu.VMEM((column, places), f32),
            pltpu.VMEM(far, bf16),
            pltpu.VMEM(far, bf16),
            pltpu.VMEM(away + near, bf16),
            pltpu.VMEM(away + near, bf16),
            pltpu.VMEM(away + far, bf16),
            pltpu.VMEM(away + far, bf16),
            pltpu.VMEM(near, i16),
            pltpu.VMEM(scale, f32),
            pltpu.VMEM(far, i16),
            pltpu.VMEM(scale, f32),
            pltpu.VMEM(away + near, i16),
            pltpu.VMEM(away + scale, f32),
            pltpu.VMEM(away + far, i16),
            pltpu.VMEM(away + scale, f32),
            pltpu.VMEM(far, i16),
            pltpu.VMEM(scale, f32),
            pltpu.VMEM(far, i16),
            pltpu.VMEM(scale, f32),
            pltpu.VMEM((rows, width, column), f32),
            pltpu.SemaphoreType.DMA(((grouped + 1) * rows + 10,)),
            pltpu.SemaphoreType.DMA((7, split_count)),
            pltpu.SemaphoreType.DMA((7, split_count)),
            pltpu.SemaphoreType.DMA((2 * grouped + 1, 8)),
            pltpu.SemaphoreType.DMA((2 * grouped + 1, 8)),
        ],
        compiler_params=pltpu.CompilerParams(
            collective_id=0, has_side_effects=True, vmem_limit_bytes=48 << 20
        ),
        name="step",
    )(
        fine_owner, obs_count,
        *[
            pltpu.with_memory_space_constraint(value, pltpu.HBM)
            for value in (
                alpha.reshape(members * levels, rows, width), chi.reshape(column, rows, width),
                perturb.reshape(members, variables, count, width), kappa, static_vert, vert_bounds,
                jacobian, obs_stencil.reshape(1, places), obs_weight, background, observed, inv_var,
            )
        ],
    )
    alpha_out, chi_out = (members * levels, rows, width), (column, rows, width)
    grad_alpha, grad_chi = pl.pallas_call(
        unpack_kernel,
        in_specs=[vmem, vmem],
        out_specs=[hbm, hbm],
        out_shape=[jax.ShapeDtypeStruct(alpha_out, f32), jax.ShapeDtypeStruct(chi_out, f32)],
        scratch_shapes=[pltpu.SemaphoreType.DMA((2, rows))],
        compiler_params=pltpu.CompilerParams(vmem_limit_bytes=16 << 20),
        name="unpack",
    )(grad_alpha, grad_chi)
    return grad_alpha.reshape(alpha.shape), grad_chi.reshape(chi.shape)


def solution(mesh):
    in_specs = (
        P("mem", None, "gy", "gx"),
        P("mem", None, None, "gy", "gx"),
        P(None, None, "gy", "gx"),
        P("gy", "gx"),
        P(),
        P(),
        P(("gy", "gx"), None),
        P(("mem", "gy", "gx")),
        P(None, ("mem", "gy", "gx")),
        P(("mem", "gy", "gx"), None),
        P(None, ("mem", "gy", "gx")),
        P(None, ("mem", "gy", "gx")),
        P(),
        P(("mem", "gy", "gx")),
    )
    out_specs = (P("mem", None, "gy", "gx"), P(None, None, "gy", "gx"))
    return jax.shard_map(body, mesh=mesh, in_specs=in_specs, out_specs=out_specs, check_vma=False)
```
